128 devices in a mesh: gy: 16 (over x_lo, z, core), gz: 8 (over y, x_hi).
Axes of the slice: x: 4 (x_hi: 2, x_lo: 2; x = x_hi * 2 + x_lo), y: 4, z: 4, core: 2. Of those that a mesh axis runs over, the one named last changes fastest.
Arguments:
- phase_field: float32 [128, 512, 1024], P('gz', 'gy'), may hold values from 0 to 1
- others: float32 [128, 512, 1024], P('gz', 'gy'), may hold values from 0 to 1
- cond_x: float32 [1023], replicated, may hold values from 256 to 4096
- cond_y: float32 [511], replicated, may hold values from 256 to 4096
- cond_z: float32 [127], replicated, may hold values from 64 to 1024
- inverse_x: float32 [1024, 1024], replicated, as said below
- inverse_y: float32 [512, 512], replicated
- inverse_z: float32 [128, 128], replicated
Outputs:
- grown: float32 [128, 512, 1024], P('gz', 'gy')
The draws below stay inside these ranges and needn't reach their ends.
Inputs may be any that keep to these rules, and one draw needn't show every extreme that they name: inverse_x is the inverse of the 1024 x 1024 matrix I - 0.5 Lx, where Lx maps a line v to cond_x[i] (v[i+1] - v[i]) - cond_x[i-1] (v[i] - v[i-1]) with the missing edges at the ends left out; inverse_y and inverse_z are built likewise from cond_y and cond_z.
All inputs are finite; a program needn't handle non-finite values.
Results may differ from the reference program's by a relative error of at most 0.0003.
Values sent between devices are 32-bit elements; how exact they have to be, the bound alone decides.
A program may use at most 128 MiB of HBM per device.

```python
import jax
import jax.numpy as jnp
from jax import lax

NX = 1024
NY = 512
NZ = 128
STEPS = 2


lateral_low = 256.0


lateral_high = 4096.0


growth_low = 64.0


growth_high = 1024.0


def line_system(key, tag, count, low, high):
    sub = jax.random.fold_in(key, tag)
    logs = jax.random.uniform(sub, (count - 1,), jnp.float32, jnp.log(low), jnp.log(high))
    weights = jnp.exp(logs)
    padded = jnp.pad(weights, (1, 1))
    diagonal = 1.0 + 0.5 * (padded[:-1] + padded[1:])
    matrix = jnp.diag(diagonal) - 0.5 * jnp.diag(weights, 1) - 0.5 * jnp.diag(weights, -1)
    inverse = jnp.linalg.solve(matrix, jnp.eye(count, dtype=jnp.float32))
    return (weights, inverse)


def draw_cond_x(key, part):
    return line_system(key, 11, NX, lateral_low, lateral_high)[0]


def draw_inverse_x(key, part):
    return line_system(key, 11, NX, lateral_low, lateral_high)[1]


def draw_cond_y(key, part):
    return line_system(key, 12, NY, lateral_low, lateral_high)[0]


def draw_inverse_y(key, part):
    return line_system(key, 12, NY, lateral_low, lateral_high)[1]


def draw_cond_z(key, part):
    return line_system(key, 13, NZ, growth_low, growth_high)[0]


def draw_inverse_z(key, part):
    return line_system(key, 13, NZ, growth_low, growth_high)[1]


def smooth_part(key):
    keys = jax.random.split(key, 2)
    waves = jax.random.randint(keys[0], (3,), 1, 5).astype(jnp.float32)
    shifts = jax.random.uniform(keys[1], (3,), jnp.float32, -3.14159, 3.14159)
    coord_z = jnp.arange(NZ, dtype=jnp.float32) / NZ
    coord_y = jnp.arange(NY, dtype=jnp.float32) / NY
    coord_x = jnp.arange(NX, dtype=jnp.float32) / NX
    wave_z = jnp.cos(6.28318 * waves[0] * coord_z + shifts[0])
    wave_y = jnp.cos(6.28318 * waves[1] * coord_y + shifts[1])
    wave_x = jnp.cos(6.28318 * waves[2] * coord_x + shifts[2])
    return wave_z[:, None, None] * wave_y[None, :, None] * wave_x[None, None, :]


def field_draw(key, tag):
    sub = jax.random.fold_in(key, tag)
    first, second = jax.random.split(sub)
    rough = jax.random.uniform(first, (NZ, NY, NX), jnp.float32, 0.0, 1.0)
    smooth = smooth_part(second)
    return 0.5 * rough + 0.25 + 0.25 * smooth


def draw_phase_field(key, part):
    return field_draw(key, 21)


def draw_others(key, part):
    return field_draw(key, 22)


def setup_inputs(seed: int = 0) -> dict:
    arg_keys = jax.random.split(jax.random.key(seed), 9)
    phase_field = draw_phase_field(jax.random.fold_in(arg_keys[8], 71), 0)
    others = draw_others(jax.random.fold_in(arg_keys[8], 71), 0)
    cond_x = draw_cond_x(jax.random.fold_in(arg_keys[8], 71), 0)
    cond_y = draw_cond_y(jax.random.fold_in(arg_keys[8], 71), 0)
    cond_z = draw_cond_z(jax.random.fold_in(arg_keys[8], 71), 0)
    inverse_x = draw_inverse_x(jax.random.fold_in(arg_keys[8], 71), 0)
    inverse_y = draw_inverse_y(jax.random.fold_in(arg_keys[8], 71), 0)
    inverse_z = draw_inverse_z(jax.random.fold_in(arg_keys[8], 71), 0)
    return {"phase_field": phase_field, "others": others, "cond_x": cond_x, "cond_y": cond_y, "cond_z": cond_z, "inverse_x": inverse_x, "inverse_y": inverse_y, "inverse_z": inverse_z}


reaction_rate = 2.0

def laplace(field, cond_x, cond_y, cond_z):
    flux_x = jnp.pad(jnp.diff(field, axis=2) * cond_x, ((0, 0), (0, 0), (1, 1)))
    flux_y = jnp.pad(jnp.diff(field, axis=1) * cond_y[:, None], ((0, 0), (1, 1), (0, 0)))
    flux_z = jnp.pad(jnp.diff(field, axis=0) * cond_z[:, None, None], ((1, 1), (0, 0), (0, 0)))
    total = flux_x[:, :, 1:] - flux_x[:, :, :-1]
    total = total + (flux_y[:, 1:, :] - flux_y[:, :-1, :])
    return total + (flux_z[1:] - flux_z[:-1])

def reference(phase_field, others, cond_x, cond_y, cond_z, inverse_x, inverse_y, inverse_z):
    field = phase_field
    for step in range(STEPS):
        lap = laplace(field, cond_x, cond_y, cond_z)
        rhs = lap + reaction_rate * (field - field * field * field - 2.0 * field * others)
        moved = jnp.einsum('zyx,wx->zyw', rhs, inverse_x, precision=lax.Precision.HIGHEST)
        moved = jnp.einsum('zyx,wy->zwx', moved, inverse_y, precision=lax.Precision.HIGHEST)
        moved = jnp.einsum('zyx,wz->wyx', moved, inverse_z, precision=lax.Precision.HIGHEST)
        field = field + moved
    return field
```

```python
import functools

import jax
import jax.numpy as jnp
from jax import lax
from jax.experimental import pallas as pl
from jax.experimental.pallas import tpu as pltpu
from jax.sharding import PartitionSpec as P

STEPS = 2
LANES = 128
SLOT = 24
F32 = jnp.float32
BF16 = jnp.bfloat16
MESH = pl.DeviceIdType.MESH


def exact(a, b):
    return jnp.dot(a, b, precision=lax.Precision.HIGHEST, preferred_element_type=F32)


def split(x):
    high = x.astype(BF16)
    return high, (x - high.astype(F32)).astype(BF16)


def product(a, b):
    dot = functools.partial(jnp.dot, preferred_element_type=F32)
    return dot(a[0], b[0]) + (dot(a[1], b[0]) + dot(a[0], b[1]))


def rows_of(shape):
    return lax.broadcasted_iota(jnp.int32, shape, 0)


def cols_of(shape):
    return lax.broadcasted_iota(jnp.int32, shape, 1)


def over_slot(i):
    return lax.shift_right_logical(i * 2731, jnp.full_like(i, 16))


def halved(i, bits):
    return lax.shift_right_logical(i, jnp.full_like(i, bits))


def onehot(mask):
    return jnp.where(mask, 1.0, 0.0).astype(F32)


def coarse(inverse, size, blocks):
    width = size * blocks
    at = cols_of((blocks, width)) - rows_of((blocks, width)) * size
    first_rows, last_rows = exact(onehot(at == 0), inverse), exact(onehot(at == size - 1), inverse)
    at = rows_of((width, blocks)) - cols_of((width, blocks)) * size
    first, last = onehot(at == 0), onehot(at == size - 1)
    i, j = rows_of((blocks, blocks)), cols_of((blocks, blocks))
    last_last = jnp.sum(jnp.where(i == j, exact(last_rows, last), 0.0), axis=0, keepdims=True)
    first_first = jnp.sum(jnp.where(i == j, exact(first_rows, first), 0.0), axis=0, keepdims=True)
    left = jnp.where(j < i, exact(first_rows, last) / last_last, 0.0)
    right = jnp.where(j > i, exact(last_rows, first) / first_first, 0.0)
    return left, right


def kernel(
    NBY, NBZ, BY, BZ, NX,
    phi_h, oth_h, gx_h, gy_h, gz_h, out_h,
    phi_v, oth_v, gx_v, gy_v, gz_v,
    gxs, ms, kz, bdy, es, kw, kwc, kcs, kzl, kzr,
    phs, pss, hs, acs, bb, loc,
    red, yrecv, zrecv, crecv, csend, yback, zback, ymain, cmat,
    load_sem, own_sem, send_sem, recv_sem,
):
    a, b = lax.axis_index("gy"), lax.axis_index("gz")
    piece, side = a // 2, a % 2
    R = BY * BZ
    by, bz = BY.bit_length() - 1, BZ.bit_length() - 1
    YM = 2 * SLOT
    MR = YM + 2 * BY
    CW = 256
    turns = NX // CW

    barrier = pltpu.get_barrier_semaphore()

    def greet_y(k, _):
        pl.semaphore_signal(barrier, inc=1, device_id=((a + k) % NBY, b), device_id_type=MESH)
        return _

    def greet_z(k, _):
        pl.semaphore_signal(barrier, inc=1, device_id=(a, (b + k) % NBZ), device_id_type=MESH)
        return _

    lax.fori_loop(1, NBY, greet_y, 0)
    lax.fori_loop(1, NBZ, greet_z, 0)

    pairs = ((gy_h, gy_v), (gz_h, gz_v), (phi_h, phi_v), (oth_h, oth_v), (gx_h, gx_v))
    loads = [pltpu.make_async_copy(s, d, load_sem.at[i]) for i, (s, d) in enumerate(pairs)]
    for load in loads:
        load.start()
    loads[0].wait()
    loads[1].wait()

    k, c = rows_of((BY * NBY, R)), cols_of((BY * NBY, R))
    gye = exact(gy_v[pl.ds(pl.multiple_of(a * BY, BY), BY), :], onehot(k == a * BY + (c & (BY - 1))))
    k, c = rows_of((BZ * NBZ, R)), cols_of((BZ * NBZ, R))
    gze = exact(gz_v[pl.ds(pl.multiple_of(b * BZ, BZ), BZ), :], onehot(k == b * BZ + halved(c, by)))
    oz = onehot(rows_of((BZ, R)) == halved(cols_of((BZ, R)), by))
    oy = onehot(rows_of((BY, R)) == (cols_of((BY, R)) & (BY - 1)))
    yl, yf = gye[BY - 1 : BY], gye[0:1]
    zl, zf = gze[BZ - 1 : BZ], gze[0:1]

    def corner(first, second):
        i = rows_of((SLOT - BZ, R))
        return jnp.where(i == 0, first, jnp.where(i == 1, second, 0.0))

    none = jnp.zeros((SLOT - BZ, R), F32)
    m_s = jnp.concatenate(
        [gze * yl, corner(zl * yl, zf * yl), gze * yf, corner(zl * yf, zf * yf), gye * zl, gye * zf], axis=0
    )
    m_t = jnp.concatenate([oz * yl, none, oz * yf, none, oy * zl, oy * zf], axis=0)
    ms[0, 0:MR], ms[1, 0:MR] = split(m_s)
    ms[0, MR:], ms[1, MR:] = split(m_t)
    ey_l, ey_r = yf / yf[:, 0:1], yl / yl[:, BY - 1 : BY]
    ez_l, ez_r = zf / zf[:, 0:1], zl / zl[:, R - BY : R - BY + 1]
    e_t = jnp.concatenate(
        [oz * ey_l, corner(ey_l * ez_l, ey_l * ez_r), oz * ey_r, corner(ey_r * ez_l, ey_r * ez_r),
         oy * ez_l, oy * ez_r], axis=0
    )
    es[0], es[1] = split(jnp.transpose(e_t))

    KR = R // 2
    i, j = rows_of((KR, KR)), cols_of((KR, KR))
    tiled = jnp.concatenate([gye[:, 0:KR]] * (KR // BY), axis=0)
    bdy[0], bdy[1] = split(jnp.where(halved(i, by) == halved(j, by), tiled, 0.0))
    half = BY // 2
    hb = by - 1
    k, c = rows_of((BZ * NBZ, KR)), cols_of((BZ * NBZ, KR))
    gzh = exact(gz_v[pl.ds(pl.multiple_of(b * BZ, BZ), BZ), :], onehot(k == b * BZ + halved(c, hb)))
    spread = exact(onehot(halved(rows_of((KR, BZ)), hb) == cols_of((KR, BZ))), gzh)
    kz[0], kz[1] = split(jnp.where((i & (half - 1)) == (j & (half - 1)), spread, 0.0))

    wl, wr = coarse(gy_v[...], BY, NBY)
    w = jnp.where(side == 0, wl, wr)
    KY = NBY * SLOT
    wide = exact(w, onehot(rows_of((NBY, KY)) == over_slot(cols_of((NBY, KY)))))
    full = exact(onehot(over_slot(rows_of((KY, NBY))) == cols_of((KY, NBY))), wide)
    i, j = rows_of((KY, KY)), cols_of((KY, KY))
    ii = i - SLOT * over_slot(i)
    kw[0], kw[1] = split(jnp.where((ii == j - SLOT * over_slot(j)) & (ii < BZ), full, 0.0))
    i, j = rows_of((2 * NBY, KY)), cols_of((2 * NBY, KY))
    kind = jnp.where(i >= NBY, 1, 0)
    pick = exact(onehot(rows_of((2 * NBY, NBY)) - NBY * jnp.where(rows_of((2 * NBY, NBY)) >= NBY, 1, 0)
                        == cols_of((2 * NBY, NBY))), wide)
    kwc[0], kwc[1] = split(jnp.where(j - SLOT * over_slot(j) == BZ + kind, pick, 0.0))

    wl, wr = coarse(gz_v[...], BZ, NBZ)
    KZ = NBZ * BY
    i, j = rows_of((KZ, KZ)), cols_of((KZ, KZ))
    same = (i & (BY - 1)) == (j & (BY - 1))
    down = onehot(halved(rows_of((KZ, NBZ)), by) == cols_of((KZ, NBZ)))
    across = onehot(rows_of((NBZ, KZ)) == halved(cols_of((NBZ, KZ)), by))
    kzl[0], kzl[1] = split(jnp.where(same, exact(down, exact(wl, across)), 0.0))
    kzr[0], kzr[1] = split(jnp.where(same, exact(down, exact(wr, across)), 0.0))
    mine = onehot(cols_of((NBZ, NBZ)) == b)
    KC = NBZ * NBY
    nb = NBY.bit_length() - 1
    across = onehot(rows_of((NBZ, KC)) == halved(cols_of((NBZ, KC)), nb))
    row_l = exact(exact(mine, wl), across)[0:1]
    row_r = exact(exact(mine, wr), across)[0:1]
    i, j = rows_of((KY, KC)), cols_of((KY, KC))
    ii = i - SLOT * over_slot(i)
    value = jnp.where(ii == BZ, row_l, jnp.where(ii == BZ + 1, row_r, 0.0))
    kcs[0], kcs[1] = split(jnp.where(over_slot(i) == (j & (NBY - 1)), value, 0.0))
    crecv[:, b] = jnp.zeros((STEPS, NBY, LANES), F32)

    loads[4].wait()

    def cut_gx(t, _):
        at = pl.ds(pl.multiple_of(t * 128, 128), 128)
        high, low = split(gx_v[at, :])
        gxs[0, at, :], gxs[1, at, :] = high, low
        return _

    lax.fori_loop(0, NX // 128, cut_gx, 0)
    loads[2].wait()
    loads[3].wait()

    def chunk(t):
        return pl.ds(pl.multiple_of(t * CW, CW), CW)

    def lanes(t):
        return pl.ds(pl.multiple_of(t * LANES, LANES), LANES)

    def pair(ref, *at):
        return ref[(0, *at)], ref[(1, *at)]

    def settle(ref, sem):
        pltpu.make_async_copy(ref, ref, sem).wait()

    everything = slice(None)

    def step(s, carry):
        def reduce(t, _):
            at = chunk(t)
            field = phi_v[:, at]
            psi = field * (8.0 - 2.0 * field * field - 4.0 * oth_v[:, at])
            ph, ps = split(field), split(psi)
            phs[0, :, at], phs[1, :, at] = ph
            pss[0, :, at], pss[1, :, at] = ps
            both = product(pair(ms), ph)
            first = product((ms[0, 0:MR], ms[1, 0:MR]), ps)
            acs[0, :, at], acs[1, :, at] = split(first - 2.0 * both[MR:])
            bb[:, at] = both[0:MR]
            return _

        lax.fori_loop(0, turns, reduce, 0)

        def reduce_x(t, _):
            at = chunk(t)
            red[s, :, at] = product(pair(acs), pair(gxs, everything, at)) - 2.0 * bb[:, at]
            return _

        lax.fori_loop(0, turns, reduce_x, 0)

        @pl.when(s == 0)
        def _():
            pl.semaphore_wait(barrier, NBY + NBZ - 2)

        def send_y(k, _):
            to = (a + k) % NBY
            pltpu.make_async_remote_copy(
                src_ref=red.at[s, pl.ds(pl.multiple_of((to % 2) * SLOT, 8), SLOT), lanes(to // 2)],
                dst_ref=yrecv.at[s, a],
                send_sem=send_sem.at[s, 0], recv_sem=recv_sem.at[s, 0],
                device_id=(to, b), device_id_type=MESH,
            ).start()
            return _

        def send_z(k, _):
            to = (b + k) % NBZ
            pltpu.make_async_remote_copy(
                src_ref=red.at[s, pl.ds(YM, 2 * BY), lanes(to)],
                dst_ref=zrecv.at[s, b],
                send_sem=send_sem.at[s, 1], recv_sem=recv_sem.at[s, 1],
                device_id=(a, to), device_id_type=MESH,
            ).start()
            return _

        lax.fori_loop(1, NBY, send_y, 0)
        lax.fori_loop(1, NBZ, send_z, 0)
        yrecv[s, a] = red[s, pl.ds(pl.multiple_of(side * SLOT, 8), SLOT), lanes(piece)]
        zrecv[s, b] = red[s, pl.ds(YM, 2 * BY), lanes(b)]

        def local(t, _):
            at = chunk(t)
            v, w = [], []
            for h in range(2):
                def rows(ref, q):
                    part = ref[q, :, at].reshape(BZ, 2, half, CW)
                    return part[:, h].reshape(KR, CW)

                v.append(product(pair(kz), (rows(phs, 0), rows(phs, 1))).reshape(BZ, half, CW))
                w.append(product(pair(kz), (rows(pss, 0), rows(pss, 1))).reshape(BZ, half, CW))
            v = jnp.concatenate(v, axis=1).reshape(R, CW)
            w = jnp.concatenate(w, axis=1).reshape(R, CW)
            field = phi_v[:, at]
            g = split(w - 2.0 * field)
            vs = split(v)
            for h in range(2):
                at_h = slice(h * KR, (h + 1) * KR)
                first = product(pair(bdy), (g[0][at_h], g[1][at_h]))
                second = product(pair(bdy), (vs[0][at_h], vs[1][at_h]))
                hs[0, at_h, at], hs[1, at_h, at] = split(first - 2.0 * v[at_h])
                loc[at_h, at] = field[at_h] - 2.0 * second
            return _

        lax.fori_loop(0, turns, local, 0)

        settle(yrecv.at[s, pl.ds(0, NBY - 1)], recv_sem.at[s, 0])
        ys = split(yrecv[s].reshape(KY, LANES))
        csend[s] = product(pair(kwc), ys)

        def send_c(k, _):
            to = (b + k) % NBZ
            which = 1 - (to - b + NBZ) // NBZ
            pltpu.make_async_remote_copy(
                src_ref=csend.at[s, pl.ds(pl.multiple_of(which * NBY, NBY), NBY)],
                dst_ref=crecv.at[s, b],
                send_sem=send_sem.at[s, 2], recv_sem=recv_sem.at[s, 2],
                device_id=(a, to), device_id_type=MESH,
            ).start()
            return _

        lax.fori_loop(1, NBZ, send_c, 0)
        ymain[...] = product(pair(kw), ys)

        settle(zrecv.at[s, pl.ds(0, NBZ - 1)], recv_sem.at[s, 1])
        for n, matrix in enumerate((kzl, kzr)):
            part = zrecv[s, :, n * BY : (n + 1) * BY].reshape(KZ, LANES)
            zback[s, :, n * BY : (n + 1) * BY] = product(pair(matrix), split(part)).reshape(NBZ, BY, LANES)

        def return_z(k, _):
            to = (b + k) % NBZ
            pltpu.make_async_remote_copy(
                src_ref=zback.at[s, to],
                dst_ref=cmat.at[s, pl.ds(YM, 2 * BY), lanes(b)],
                send_sem=send_sem.at[s, 3], recv_sem=recv_sem.at[s, 3],
                device_id=(a, to), device_id_type=MESH,
            ).start()
            return _

        lax.fori_loop(1, NBZ, return_z, 0)
        cmat[s, pl.ds(YM, 2 * BY), lanes(b)] = zback[s, b]

        settle(crecv.at[s, pl.ds(0, NBZ - 1)], recv_sem.at[s, 2])
        corners = product(pair(kcs), split(crecv[s].reshape(KC, LANES)))
        yback[s] = (ymain[...] + corners).reshape(NBY, SLOT, LANES)

        def return_y(k, _):
            to = (a + k) % NBY
            pltpu.make_async_remote_copy(
                src_ref=yback.at[s, to],
                dst_ref=cmat.at[s, pl.ds(pl.multiple_of(side * SLOT, 8), SLOT), lanes(piece)],
                send_sem=send_sem.at[s, 4], recv_sem=recv_sem.at[s, 4],
                device_id=(to, b), device_id_type=MESH,
            ).start()
            return _

        lax.fori_loop(1, NBY, return_y, 0)
        cmat[s, pl.ds(pl.multiple_of(side * SLOT, 8), SLOT), lanes(piece)] = yback[s, a]

        def local_x(t, _):
            at = chunk(t)
            loc[:, at] += product(pair(hs), pair(gxs, everything, at))
            return _

        lax.fori_loop(0, turns, local_x, 0)

        settle(zrecv.at[s, pl.ds(0, NBZ - 1)], recv_sem.at[s, 3])
        settle(yrecv.at[s, pl.ds(0, NBY - 1)], recv_sem.at[s, 4])

        def add(t, _):
            at = chunk(t)
            phi_v[:, at] = loc[:, at] + product(pair(es), split(cmat[s, :, at]))
            return _

        lax.fori_loop(0, turns, add, 0)
        for n in (0, 4):
            settle(yrecv.at[s, pl.ds(0, NBY - 1)], send_sem.at[s, n])
        for n in (1, 3):
            settle(zrecv.at[s, pl.ds(0, NBZ - 1)], send_sem.at[s, n])
        settle(crecv.at[s, pl.ds(0, NBZ - 1)], send_sem.at[s, 2])
        return carry

    lax.fori_loop(0, STEPS, step, 0)
    store = pltpu.make_async_copy(phi_v, out_h, own_sem)
    store.start()
    store.wait()


def body(NBY, NBZ, phase_field, others, cond_x, cond_y, cond_z, inverse_x, inverse_y, inverse_z):
    BZ, BY, NX = phase_field.shape
    R = BY * BZ
    MR = 2 * SLOT + 2 * BY
    KR, KY, KZ, KC = R // 2, NBY * SLOT, NBZ * BY, NBZ * NBY
    vmem = pltpu.VMEM
    call = pl.pallas_call(
        functools.partial(kernel, NBY, NBZ, BY, BZ, NX),
        out_shape=jax.ShapeDtypeStruct((R, NX), F32),
        in_specs=[pl.BlockSpec(memory_space=pl.ANY)] * 5,
        out_specs=pl.BlockSpec(memory_space=pl.ANY),
        scratch_shapes=[
            vmem((R, NX), F32), vmem((R, NX), F32), vmem((NX, NX), F32),
            vmem((BY * NBY, BY * NBY), F32), vmem((BZ * NBZ, BZ * NBZ), F32),
            vmem((2, NX, NX), BF16), vmem((2, 2 * MR, R), BF16), vmem((2, KR, KR), BF16),
            vmem((2, KR, KR), BF16), vmem((2, R, MR), BF16), vmem((2, KY, KY), BF16),
            vmem((2, 2 * NBY, KY), BF16), vmem((2, KY, KC), BF16), vmem((2, KZ, KZ), BF16),
            vmem((2, KZ, KZ), BF16),
            vmem((2, R, NX), BF16), vmem((2, R, NX), BF16), vmem((2, R, NX), BF16),
            vmem((2, MR, NX), BF16), vmem((MR, NX), F32), vmem((R, NX), F32),
            vmem((STEPS, MR, NX), F32), vmem((STEPS, NBY, SLOT, LANES), F32),
            vmem((STEPS, NBZ, 2 * BY, LANES), F32), vmem((STEPS, NBZ, NBY, LANES), F32),
            vmem((STEPS, 2 * NBY, LANES), F32), vmem((STEPS, NBY, SLOT, LANES), F32),
            vmem((STEPS, NBZ, 2 * BY, LANES), F32), vmem((KY, LANES), F32),
            vmem((STEPS, MR, NX), F32),
            pltpu.SemaphoreType.DMA((5,)), pltpu.SemaphoreType.DMA,
            pltpu.SemaphoreType.DMA((STEPS, 5)), pltpu.SemaphoreType.DMA((STEPS, 5)),
        ],
        compiler_params=pltpu.CompilerParams(
            collective_id=0, has_side_effects=True, vmem_limit_bytes=56 << 20
        ),
        name="adi",
    )
    out = call(
        phase_field.reshape(R, NX), others.reshape(R, NX), inverse_x, inverse_y, inverse_z
    )
    return out.reshape(BZ, BY, NX)


def solution(mesh):
    placed = (P("gz", "gy", None), P("gz", "gy", None), P(), P(), P(), P(), P(), P())
    return jax.shard_map(
        functools.partial(body, mesh.shape["gy"], mesh.shape["gz"]),
        mesh=mesh, in_specs=placed, out_specs=P("gz", "gy", None), check_vma=False,
    )
```

```python
import functools

import jax
import jax.numpy as jnp
from jax import lax
from jax.experimental import pallas as pl
from jax.experimental.pallas import tpu as pltpu
from jax.sharding import PartitionSpec as P

STEPS = 2
LANES = 128
SLOT = 24
F32 = jnp.float32
BF16 = jnp.bfloat16
MESH = pl.DeviceIdType.MESH


def exact(a, b):
    return jnp.dot(a, b, precision=lax.Precision.HIGHEST, preferred_element_type=F32)


def split(x):
    high = x.astype(BF16)
    return high, (x - high.astype(F32)).astype(BF16)


def product(a, b):
    dot = functools.partial(jnp.dot, preferred_element_type=F32)
    return dot(a[0], b[0]) + (dot(a[1], b[0]) + dot(a[0], b[1]))


def rows_of(shape):
    return lax.broadcasted_iota(jnp.int32, shape, 0)


def cols_of(shape):
    return lax.broadcasted_iota(jnp.int32, shape, 1)


def over_slot(i):
    return lax.shift_right_logical(i * 2731, jnp.full_like(i, 16))


def halved(i, bits):
    return lax.shift_right_logical(i, jnp.full_like(i, bits))


def onehot(mask):
    return jnp.where(mask, 1.0, 0.0).astype(F32)


def coarse(inverse, size, blocks):
    width = size * blocks
    at = cols_of((blocks, width)) - rows_of((blocks, width)) * size
    first_rows, last_rows = exact(onehot(at == 0), inverse), exact(onehot(at == size - 1), inverse)
    at = rows_of((width, blocks)) - cols_of((width, blocks)) * size
    first, last = onehot(at == 0), onehot(at == size - 1)
    i, j = rows_of((blocks, blocks)), cols_of((blocks, blocks))
    last_last = jnp.sum(jnp.where(i == j, exact(last_rows, last), 0.0), axis=0, keepdims=True)
    first_first = jnp.sum(jnp.where(i == j, exact(first_rows, first), 0.0), axis=0, keepdims=True)
    left = jnp.where(j < i, exact(first_rows, last) / last_last, 0.0)
    right = jnp.where(j > i, exact(last_rows, first) / first_first, 0.0)
    return left, right


def kernel(
    NBY, NBZ, BY, BZ, NX,
    phi_h, oth_h, gx_h, gy_h, gz_h, loc_h, cmat_h, ty_h, tz_h,
    phi_v, oth_v, gx_v, edge_v, gy_v, gz_v, gye_v, gze_v,
    gxs, ms, kz, bdy, ty, tz, kw, kwc, kcs, kzl, kzr,
    phs, pss, hs, acs, bb, loc,
    red, yrecv, zrecv, crecv, csend, yback, zback, ymain, cmat,
    load_sem, own_sem, send_sem, recv_sem,
):
    a, b = lax.axis_index("gy"), lax.axis_index("gz")
    piece, side = a // 2, a % 2
    R = BY * BZ
    by, bz = BY.bit_length() - 1, BZ.bit_length() - 1
    YM = 2 * SLOT
    MR = YM + 2 * BY
    CW = 256
    turns = NX // CW

    barrier = pltpu.get_barrier_semaphore()

    def greet_y(k, _):
        pl.semaphore_signal(barrier, inc=1, device_id=((a + k) % NBY, b), device_id_type=MESH)
        return _

    def greet_z(k, _):
        pl.semaphore_signal(barrier, inc=1, device_id=(a, (b + k) % NBZ), device_id_type=MESH)
        return _

    lax.fori_loop(1, NBY, greet_y, 0)
    lax.fori_loop(1, NBZ, greet_z, 0)

    pairs = [(gy_h, gy_v), (gz_h, gz_v), (phi_h, phi_v), (oth_h, oth_v)]
    for n in range(turns):
        pairs.append((gx_h.at[pl.ds(n * CW, CW), pl.ds(n * CW, CW)], gx_v.at[n]))
    for n in range(turns - 1):
        pairs.append((gx_h.at[pl.ds((n + 1) * CW - 8, 16)], edge_v.at[n]))
    loads = [pltpu.make_async_copy(s, d, load_sem.at[i]) for i, (s, d) in enumerate(pairs)]
    for load in loads:
        load.start()
    loads[0].wait()
    loads[1].wait()

    wide = min(LANES, BY * NBY)
    start = (a * BY // wide) * wide
    k, c = rows_of((wide, R)), cols_of((wide, R))
    gye = exact(
        gy_v[pl.ds(pl.multiple_of(a * BY, BY), BY), pl.ds(pl.multiple_of(start, wide), wide)],
        onehot(k == a * BY - start + (c & (BY - 1))),
    )
    k, c = rows_of((BZ * NBZ, R)), cols_of((BZ * NBZ, R))
    gze = exact(gz_v[pl.ds(pl.multiple_of(b * BZ, BZ), BZ), :], onehot(k == b * BZ + halved(c, by)))
    gye_v[...], gze_v[...] = gye, gze
    oz = onehot(rows_of((BZ, R)) == halved(cols_of((BZ, R)), by))
    oy = onehot(rows_of((BY, R)) == (cols_of((BY, R)) & (BY - 1)))
    yl, yf = gye[BY - 1 : BY], gye[0:1]
    zl, zf = gze[BZ - 1 : BZ], gze[0:1]

    def corner(first, second):
        i = rows_of((SLOT - BZ, R))
        return jnp.where(i == 0, first, jnp.where(i == 1, second, 0.0))

    none = jnp.zeros((SLOT - BZ, R), F32)
    m_s = jnp.concatenate(
        [gze * yl, corner(zl * yl, zf * yl), gze * yf, corner(zl * yf, zf * yf), gye * zl, gye * zf], axis=0
    )
    m_t = jnp.concatenate([oz * yl, none, oz * yf, none, oy * zl, oy * zf], axis=0)
    ms[0, 0:MR], ms[1, 0:MR] = split(m_s)
    ms[0, MR:], ms[1, MR:] = split(m_t)

    KR = R // 2
    half = BY // 2
    hb = by - 1
    KY, KZ, KC = NBY * SLOT, NBZ * BY, NBZ * NBY

    def more_tables():
        gye, gze = gye_v[...], gze_v[...]
        ty[0] = jnp.broadcast_to(gye[:, 0:1] / gye[0:1, 0:1], (BY, LANES))
        ty[1] = jnp.broadcast_to(gye[:, BY - 1 : BY] / gye[BY - 1 : BY, BY - 1 : BY], (BY, LANES))
        last = R - BY
        tz[0] = jnp.broadcast_to(gze[:, 0:1] / gze[0:1, 0:1], (BZ, LANES))
        tz[1] = jnp.broadcast_to(gze[:, last : last + 1] / gze[BZ - 1 : BZ, last : last + 1], (BZ, LANES))

        i, j = rows_of((KR, KR)), cols_of((KR, KR))
        tiled = jnp.concatenate([gye[:, 0:KR]] * (KR // BY), axis=0)
        bdy[0], bdy[1] = split(jnp.where(halved(i, by) == halved(j, by), tiled, 0.0))
        k, c = rows_of((BZ * NBZ, KR)), cols_of((BZ * NBZ, KR))
        gzh = exact(gz_v[pl.ds(pl.multiple_of(b * BZ, BZ), BZ), :], onehot(k == b * BZ + halved(c, hb)))
        spread = exact(onehot(halved(rows_of((KR, BZ)), hb) == cols_of((KR, BZ))), gzh)
        kz[0], kz[1] = split(jnp.where((i & (half - 1)) == (j & (half - 1)), spread, 0.0))

        wl, wr = coarse(gy_v[...], BY, NBY)
        w = jnp.where(side == 0, wl, wr)
        wide = exact(w, onehot(rows_of((NBY, KY)) == over_slot(cols_of((NBY, KY)))))
        full = exact(onehot(over_slot(rows_of((KY, NBY))) == cols_of((KY, NBY))), wide)
        i, j = rows_of((KY, KY)), cols_of((KY, KY))
        ii = i - SLOT * over_slot(i)
        kw[0], kw[1] = split(jnp.where((ii == j - SLOT * over_slot(j)) & (ii < BZ), full, 0.0))
        i, j = rows_of((2 * NBY, KY)), cols_of((2 * NBY, KY))
        kind = jnp.where(i >= NBY, 1, 0)
        pick = exact(onehot(rows_of((2 * NBY, NBY)) - NBY * jnp.where(rows_of((2 * NBY, NBY)) >= NBY, 1, 0)
                            == cols_of((2 * NBY, NBY))), wide)
        kwc[0], kwc[1] = split(jnp.where(j - SLOT * over_slot(j) == BZ + kind, pick, 0.0))

        wl, wr = coarse(gz_v[...], BZ, NBZ)
        i, j = rows_of((KZ, KZ)), cols_of((KZ, KZ))
        same = (i & (BY - 1)) == (j & (BY - 1))
        down = onehot(halved(rows_of((KZ, NBZ)), by) == cols_of((KZ, NBZ)))
        across = onehot(rows_of((NBZ, KZ)) == halved(cols_of((NBZ, KZ)), by))
        kzl[0], kzl[1] = split(jnp.where(same, exact(down, exact(wl, across)), 0.0))
        kzr[0], kzr[1] = split(jnp.where(same, exact(down, exact(wr, across)), 0.0))
        mine = onehot(cols_of((NBZ, NBZ)) == b)
        nb = NBY.bit_length() - 1
        across = onehot(rows_of((NBZ, KC)) == halved(cols_of((NBZ, KC)), nb))
        row_l = exact(exact(mine, wl), across)[0:1]
        row_r = exact(exact(mine, wr), across)[0:1]
        i, j = rows_of((KY, KC)), cols_of((KY, KC))
        ii = i - SLOT * over_slot(i)
        value = jnp.where(ii == BZ, row_l, jnp.where(ii == BZ + 1, row_r, 0.0))
        kcs[0], kcs[1] = split(jnp.where(over_slot(i) == (j & (NBY - 1)), value, 0.0))

    crecv[:, b] = jnp.zeros((STEPS, NBY, LANES), F32)
    for load in loads[4:]:
        load.wait()
    for n in range(turns):
        gxs[0, n], gxs[1, n] = split(gx_v[n])
    loads[2].wait()
    loads[3].wait()

    def chunk(t):
        return pl.ds(pl.multiple_of(t * CW, CW), CW)

    def lanes(t):
        return pl.ds(pl.multiple_of(t * LANES, LANES), LANES)

    def pair(ref, *at):
        return ref[(0, *at)], ref[(1, *at)]

    def settle(ref, sem):
        pltpu.make_async_copy(ref, ref, sem).wait()

    def along_x(source, target, rows, extra):
        first, last = [], []
        for n in range(turns):
            at = slice(n * CW, (n + 1) * CW)
            part = product((source[0, rows, at], source[1, rows, at]), pair(gxs, n))
            target[rows, at] = part + extra(at)
            first.append(part[:, 0:1])
            last.append(part[:, CW - 1 : CW])
        ups, downs = [None] * turns, [None] * turns
        carry = last[0]
        for n in range(1, turns):
            edge = edge_v[n - 1, 7:8, n * CW : (n + 1) * CW] / edge_v[n - 1, 7:8, n * CW - 1 : n * CW]
            ups[n] = (carry, edge)
            carry = last[n] + carry * edge[:, CW - 1 : CW]
        carry = first[turns - 1]
        for n in range(turns - 2, -1, -1):
            at = (n + 1) * CW
            edge = edge_v[n, 8:9, n * CW : at] / edge_v[n, 8:9, at : at + 1]
            downs[n] = (carry, edge)
            carry = first[n] + carry * edge[:, 0:1]
        for n in range(turns):
            at = slice(n * CW, (n + 1) * CW)
            terms = [p[0] * p[1] for p in (ups[n], downs[n]) if p is not None]
            if terms:
                target[rows, at] += sum(terms[1:], terms[0])

    def prepare(field, at):
        psi = field * (8.0 - 2.0 * field * field - 4.0 * oth_v[at])
        phs[(0, *at)], phs[(1, *at)] = split(field)
        pss[(0, *at)], pss[(1, *at)] = split(psi)

    def prepare_rows(z, _):
        at = (pl.ds(pl.multiple_of(z * BY, BY), BY), slice(None))
        prepare(phi_v[at], at)
        return _

    lax.fori_loop(0, BZ, prepare_rows, 0)

    def step(s, carry):
        def reduce(t, _):
            at = chunk(t)
            both = product(pair(ms), (phs[0, :, at], phs[1, :, at]))
            first = product((ms[0, 0:MR], ms[1, 0:MR]), (pss[0, :, at], pss[1, :, at]))
            acs[0, :, at], acs[1, :, at] = split(first - 2.0 * both[MR:])
            bb[:, at] = -2.0 * both[0:MR]
            return _

        lax.fori_loop(0, turns, reduce, 0)
        along_x(acs, red.at[s], slice(0, MR), lambda at: bb[:, at])

        @pl.when(s == 0)
        def _():
            pl.semaphore_wait(barrier, NBY + NBZ - 2)

        def send_y(k, _):
            to = (a + k) % NBY
            pltpu.make_async_remote_copy(
                src_ref=red.at[s, pl.ds(pl.multiple_of((to % 2) * SLOT, 8), SLOT), lanes(to // 2)],
                dst_ref=yrecv.at[s, a],
                send_sem=send_sem.at[s, 0], recv_sem=recv_sem.at[s, 0],
                device_id=(to, b), device_id_type=MESH,
            ).start()
            return _

        def send_z(k, _):
            to = (b + k) % NBZ
            pltpu.make_async_remote_copy(
                src_ref=red.at[s, pl.ds(YM, 2 * BY), lanes(to)],
                dst_ref=zrecv.at[s, b],
                send_sem=send_sem.at[s, 1], recv_sem=recv_sem.at[s, 1],
                device_id=(a, to), device_id_type=MESH,
            ).start()
            return _

        lax.fori_loop(1, NBY, send_y, 0)
        lax.fori_loop(1, NBZ, send_z, 0)
        yrecv[s, a] = red[s, pl.ds(pl.multiple_of(side * SLOT, 8), SLOT), lanes(piece)]
        zrecv[s, b] = red[s, pl.ds(YM, 2 * BY), lanes(b)]

        @pl.when(s == 0)
        def _():
            more_tables()

        settle(yrecv.at[s, pl.ds(0, NBY - 1)], recv_sem.at[s, 0])
        ys = split(yrecv[s].reshape(KY, LANES))
        csend[s] = product(pair(kwc), ys)

        def send_c(k, _):
            to = (b + k) % NBZ
            which = 1 - (to - b + NBZ) // NBZ
            pltpu.make_async_remote_copy(
                src_ref=csend.at[s, pl.ds(pl.multiple_of(which * NBY, NBY), NBY)],
                dst_ref=crecv.at[s, b],
                send_sem=send_sem.at[s, 2], recv_sem=recv_sem.at[s, 2],
                device_id=(a, to), device_id_type=MESH,
            ).start()
            return _

        lax.fori_loop(1, NBZ, send_c, 0)
        ymain[...] = product(pair(kw), ys)

        settle(zrecv.at[s, pl.ds(0, NBZ - 1)], recv_sem.at[s, 1])
        for n, matrix in enumerate((kzl, kzr)):
            part = zrecv[s, :, n * BY : (n + 1) * BY].reshape(KZ, LANES)
            zback[s, :, n * BY : (n + 1) * BY] = product(pair(matrix), split(part)).reshape(NBZ, BY, LANES)

        def return_z(k, _):
            to = (b + k) % NBZ
            pltpu.make_async_remote_copy(
                src_ref=zback.at[s, to],
                dst_ref=cmat.at[s, pl.ds(YM, 2 * BY), lanes(b)],
                send_sem=send_sem.at[s, 3], recv_sem=recv_sem.at[s, 3],
                device_id=(a, to), device_id_type=MESH,
            ).start()
            return _

        lax.fori_loop(1, NBZ, return_z, 0)
        cmat[s, pl.ds(YM, 2 * BY), lanes(b)] = zback[s, b]

        def local(t, _):
            at = chunk(t)
            v, w = [], []
            for h in range(2):
                def rows(ref, q):
                    part = ref[q, :, at].reshape(BZ, 2, half, CW)
                    return part[:, h].reshape(KR, CW)

                v.append(product(pair(kz), (rows(phs, 0), rows(phs, 1))).reshape(BZ, half, CW))
                w.append(product(pair(kz), (rows(pss, 0), rows(pss, 1))).reshape(BZ, half, CW))
            v = jnp.concatenate(v, axis=1).reshape(R, CW)
            w = jnp.concatenate(w, axis=1).reshape(R, CW)
            field = phi_v[:, at]
            g = split(w - 2.0 * field)
            vs = split(v)
            for h in range(2):
                at_h = slice(h * KR, (h + 1) * KR)
                first = product(pair(bdy), (g[0][at_h], g[1][at_h]))
                second = product(pair(bdy), (vs[0][at_h], vs[1][at_h]))
                hs[0, at_h, at], hs[1, at_h, at] = split(first - 2.0 * v[at_h])
                loc[at_h, at] = field[at_h] - 2.0 * second
            return _

        lax.fori_loop(0, turns, local, 0)

        settle(crecv.at[s, pl.ds(0, NBZ - 1)], recv_sem.at[s, 2])
        corners = product(pair(kcs), split(crecv[s].reshape(KC, LANES)))
        yback[s] = (ymain[...] + corners).reshape(NBY, SLOT, LANES)

        def return_y(k, _):
            to = (a + k) % NBY
            pltpu.make_async_remote_copy(
                src_ref=yback.at[s, to],
                dst_ref=cmat.at[s, pl.ds(pl.multiple_of(side * SLOT, 8), SLOT), lanes(piece)],
                send_sem=send_sem.at[s, 4], recv_sem=recv_sem.at[s, 4],
                device_id=(to, b), device_id_type=MESH,
            ).start()
            return _

        lax.fori_loop(1, NBY, return_y, 0)
        cmat[s, pl.ds(pl.multiple_of(side * SLOT, 8), SLOT), lanes(piece)] = yback[s, a]

        def local_x(t, _):
            rows = pl.ds(pl.multiple_of(t * 128, 128), 128)
            along_x(hs, loc, rows, lambda at: loc[rows, at])
            return _

        lax.fori_loop(0, R // 128, local_x, 0)

        @pl.when(s == STEPS - 1)
        def _():
            pltpu.make_async_copy(loc, loc_h, own_sem.at[0]).start()

        settle(zrecv.at[s, pl.ds(0, NBZ - 1)], recv_sem.at[s, 3])
        settle(yrecv.at[s, pl.ds(0, NBY - 1)], recv_sem.at[s, 4])

        @pl.when(s < STEPS - 1)
        def _():
            def add(c, _):
                at = lanes(c)
                sums = [cmat[s, r : r + n, at] for r, n in parts(BY, BZ)]
                expand(BY, BZ, sums, ty, tz, lambda rows: loc[rows, at], lambda rows, v: put(rows, at, v))
                return _

            def put(rows, at, value):
                phi_v[rows, at] = value
                prepare(value, (rows, at))

            lax.fori_loop(0, NX // LANES, add, 0)

        @pl.when(s == STEPS - 1)
        def _():
            pltpu.make_async_copy(cmat.at[s], cmat_h, own_sem.at[1]).start()

        for n in (0, 4):
            settle(yrecv.at[s, pl.ds(0, NBY - 1)], send_sem.at[s, n])
        for n in (1, 3):
            settle(zrecv.at[s, pl.ds(0, NBZ - 1)], send_sem.at[s, n])
        settle(crecv.at[s, pl.ds(0, NBZ - 1)], send_sem.at[s, 2])
        return carry

    lax.fori_loop(0, STEPS, step, 0)
    ends = ((loc, loc_h), (cmat.at[STEPS - 1], cmat_h), (ty, ty_h), (tz, tz_h))
    ends = [pltpu.make_async_copy(x, y, own_sem.at[n]) for n, (x, y) in enumerate(ends)]
    ends[2].start()
    ends[3].start()
    for end in ends:
        end.wait()


def parts(BY, BZ):
    return (0, BZ), (BZ, 1), (BZ + 1, 1), (SLOT, BZ), (SLOT + BZ, 1), (SLOT + BZ + 1, 1), \
        (2 * SLOT, BY), (2 * SLOT + BY, BY)


def expand(BY, BZ, sums, ty, tz, get, put, planes=None):
    yl, cll, clr, yr, crl, crr, zl, zr = sums
    tl, tr = ty[0], ty[1]
    zl = zl + tl * cll + tr * crl
    zr = zr + tl * clr + tr * crr
    for z in range(BZ):
        rows = slice(z * BY, (z + 1) * BY)
        ends = tl * yl[z : z + 1] + tr * yr[z : z + 1]
        put(rows, get(rows) + ends + tz[0, z : z + 1] * zl + tz[1, z : z + 1] * zr)


def finish(BY, BZ, loc, cmat, ty, tz, out):
    sums = [cmat[r : r + n, :] for r, n in parts(BY, BZ)]

    def put(rows, value):
        out[rows, :] = value

    expand(BY, BZ, sums, ty, tz, lambda rows: loc[rows, :], put)


def body(NBY, NBZ, phase_field, others, cond_x, cond_y, cond_z, inverse_x, inverse_y, inverse_z):
    BZ, BY, NX = phase_field.shape
    R = BY * BZ
    MR = 2 * SLOT + 2 * BY
    KR, KY, KZ, KC = R // 2, NBY * SLOT, NBZ * BY, NBZ * NBY
    vmem = pltpu.VMEM
    CW, turns = 256, NX // 256
    call = pl.pallas_call(
        functools.partial(kernel, NBY, NBZ, BY, BZ, NX),
        out_shape=[
            jax.ShapeDtypeStruct((R, NX), F32), jax.ShapeDtypeStruct((MR, NX), F32),
            jax.ShapeDtypeStruct((2, BY, LANES), F32), jax.ShapeDtypeStruct((2, BZ, LANES), F32),
        ],
        in_specs=[pl.BlockSpec(memory_space=pl.ANY)] * 5,
        out_specs=[pl.BlockSpec(memory_space=pl.ANY)] * 4,
        scratch_shapes=[
            vmem((R, NX), F32), vmem((R, NX), F32), vmem((turns, CW, CW), F32),
            vmem((max(turns - 1, 1), 16, NX), F32),
            vmem((BY * NBY, BY * NBY), F32), vmem((BZ * NBZ, BZ * NBZ), F32),
            vmem((BY, R), F32), vmem((BZ, R), F32),
            vmem((2, turns, CW, CW), BF16), vmem((2, 2 * MR, R), BF16), vmem((2, KR, KR), BF16),
            vmem((2, KR, KR), BF16), vmem((2, BY, LANES), F32), vmem((2, BZ, LANES), F32),
            vmem((2, KY, KY), BF16),
            vmem((2, 2 * NBY, KY), BF16), vmem((2, KY, KC), BF16), vmem((2, KZ, KZ), BF16),
            vmem((2, KZ, KZ), BF16),
            vmem((2, R, NX), BF16), vmem((2, R, NX), BF16), vmem((2, R, NX), BF16),
            vmem((2, MR, NX), BF16), vmem((MR, NX), F32), vmem((R, NX), F32),
            vmem((STEPS, MR, NX), F32), vmem((STEPS, NBY, SLOT, LANES), F32),
            vmem((STEPS, NBZ, 2 * BY, LANES), F32), vmem((STEPS, NBZ, NBY, LANES), F32),
            vmem((STEPS, 2 * NBY, LANES), F32), vmem((STEPS, NBY, SLOT, LANES), F32),
            vmem((STEPS, NBZ, 2 * BY, LANES), F32), vmem((KY, LANES), F32),
            vmem((STEPS, MR, NX), F32),
            pltpu.SemaphoreType.DMA((2 * turns + 3,)), pltpu.SemaphoreType.DMA((4,)),
            pltpu.SemaphoreType.DMA((STEPS, 5)), pltpu.SemaphoreType.DMA((STEPS, 5)),
        ],
        compiler_params=pltpu.CompilerParams(
            collective_id=0, has_side_effects=True, vmem_limit_bytes=56 << 20
        ),
        name="adi",
    )
    loc, cmat, ty, tz = call(
        phase_field.reshape(R, NX), others.reshape(R, NX), inverse_x, inverse_y, inverse_z
    )
    out = pl.pallas_call(
        functools.partial(finish, BY, BZ),
        out_shape=jax.ShapeDtypeStruct((R, NX), F32),
        grid=(NX // LANES,),
        in_specs=[
            pl.BlockSpec((R, LANES), lambda c: (0, c)), pl.BlockSpec((MR, LANES), lambda c: (0, c)),
            pl.BlockSpec((2, BY, LANES), lambda c: (0, 0, 0)), pl.BlockSpec((2, BZ, LANES), lambda c: (0, 0, 0)),
        ],
        out_specs=pl.BlockSpec((R, LANES), lambda c: (0, c)),
        name="finish",
    )(loc, cmat, ty, tz)
    return out.reshape(BZ, BY, NX)


def solution(mesh):
    placed = (P("gz", "gy", None), P("gz", "gy", None), P(), P(), P(), P(), P(), P())
    return jax.shard_map(
        functools.partial(body, mesh.shape["gy"], mesh.shape["gz"]),
        mesh=mesh, in_specs=placed, out_specs=P("gz", "gy", None), check_vma=False,
    )
```

```python
import functools

import jax
import jax.numpy as jnp
from jax import lax
from jax.experimental import pallas as pl
from jax.experimental.pallas import tpu as pltpu
from jax.sharding import PartitionSpec as P

STEPS = 2
LANES = 128
SLOT = 24
F32 = jnp.float32
BF16 = jnp.bfloat16
MESH = pl.DeviceIdType.MESH


def exact(a, b):
    return jnp.dot(a, b, precision=lax.Precision.HIGHEST, preferred_element_type=F32)


def split(x):
    high = x.astype(BF16)
    return high, (x - high.astype(F32)).astype(BF16)


def product(a, b):
    dot = functools.partial(jnp.dot, preferred_element_type=F32)
    return dot(a[0], b[0]) + (dot(a[1], b[0]) + dot(a[0], b[1]))


def rows_of(shape):
    return lax.broadcasted_iota(jnp.int32, shape, 0)


def cols_of(shape):
    return lax.broadcasted_iota(jnp.int32, shape, 1)


def over_slot(i):
    return lax.shift_right_logical(i * 2731, jnp.full_like(i, 16))


def halved(i, bits):
    return lax.shift_right_logical(i, jnp.full_like(i, bits))


def onehot(mask):
    return jnp.where(mask, 1.0, 0.0).astype(F32)


def coarse(inverse, size, blocks):
    width = size * blocks
    at = cols_of((blocks, width)) - rows_of((blocks, width)) * size
    first_rows, last_rows = exact(onehot(at == 0), inverse), exact(onehot(at == size - 1), inverse)
    at = rows_of((width, blocks)) - cols_of((width, blocks)) * size
    first, last = onehot(at == 0), onehot(at == size - 1)
    i, j = rows_of((blocks, blocks)), cols_of((blocks, blocks))
    last_last = jnp.sum(jnp.where(i == j, exact(last_rows, last), 0.0), axis=0, keepdims=True)
    first_first = jnp.sum(jnp.where(i == j, exact(first_rows, first), 0.0), axis=0, keepdims=True)
    left = jnp.where(j < i, exact(first_rows, last) / last_last, 0.0)
    right = jnp.where(j > i, exact(last_rows, first) / first_first, 0.0)
    return left, right


def kernel(
    NBY, NBZ, BY, BZ, NX,
    phi_h, oth_h, gx_h, gy_h, gz_h, loc_h, yl_h, yr_h, zl_h, zr_h, tyl_h, tyr_h, tzl_h, tzr_h,
    phi_v, oth_v, gx_v, edge_v, gy_v, gz_v, gye_v, gze_v,
    gxs, ms, kz, bdy, ty, tz, kw, kwc, kcs, kzl, kzr,
    phs, pss, hs, acs, bb, loc,
    red, yrecv, zrecv, crecv, csend, yback, zback, ymain, cmat,
    load_sem, own_sem, send_sem, recv_sem,
):
    a, b = lax.axis_index("gy"), lax.axis_index("gz")
    piece, side = a // 2, a % 2
    R = BY * BZ
    by, bz = BY.bit_length() - 1, BZ.bit_length() - 1
    YM = 2 * SLOT
    MR = YM + 2 * BY
    CW = 256
    turns = NX // CW

    barrier = pltpu.get_barrier_semaphore()

    def greet_y(k, _):
        pl.semaphore_signal(barrier, inc=1, device_id=((a + k) % NBY, b), device_id_type=MESH)
        return _

    def greet_z(k, _):
        pl.semaphore_signal(barrier, inc=1, device_id=(a, (b + k) % NBZ), device_id_type=MESH)
        return _

    lax.fori_loop(1, NBY, greet_y, 0)
    lax.fori_loop(1, NBZ, greet_z, 0)

    pairs = [(gy_h, gy_v), (gz_h, gz_v), (phi_h, phi_v), (oth_h, oth_v)]
    for n in range(turns):
        pairs.append((gx_h.at[pl.ds(n * CW, CW), pl.ds(n * CW, CW)], gx_v.at[n]))
    for n in range(turns - 1):
        pairs.append((gx_h.at[pl.ds((n + 1) * CW - 8, 16)], edge_v.at[n]))
    loads = [pltpu.make_async_copy(s, d, load_sem.at[i]) for i, (s, d) in enumerate(pairs)]
    for load in loads:
        load.start()
    loads[0].wait()
    loads[1].wait()

    wide = min(LANES, BY * NBY)
    start = (a * BY // wide) * wide
    k, c = rows_of((wide, R)), cols_of((wide, R))
    gye = exact(
        gy_v[pl.ds(pl.multiple_of(a * BY, BY), BY), pl.ds(pl.multiple_of(start, wide), wide)],
        onehot(k == a * BY - start + (c & (BY - 1))),
    )
    k, c = rows_of((BZ * NBZ, R)), cols_of((BZ * NBZ, R))
    gze = exact(gz_v[pl.ds(pl.multiple_of(b * BZ, BZ), BZ), :], onehot(k == b * BZ + halved(c, by)))
    gye_v[...], gze_v[...] = gye, gze
    oz = onehot(rows_of((BZ, R)) == halved(cols_of((BZ, R)), by))
    oy = onehot(rows_of((BY, R)) == (cols_of((BY, R)) & (BY - 1)))
    yl, yf = gye[BY - 1 : BY], gye[0:1]
    zl, zf = gze[BZ - 1 : BZ], gze[0:1]

    def corner(first, second):
        i = rows_of((SLOT - BZ, R))
        return jnp.where(i == 0, first, jnp.where(i == 1, second, 0.0))

    none = jnp.zeros((SLOT - BZ, R), F32)
    m_s = jnp.concatenate(
        [gze * yl, corner(zl * yl, zf * yl), gze * yf, corner(zl * yf, zf * yf), gye * zl, gye * zf], axis=0
    )
    m_t = jnp.concatenate([oz * yl, none, oz * yf, none, oy * zl, oy * zf], axis=0)
    ms[0, 0:MR], ms[1, 0:MR] = split(m_s)
    ms[0, MR:], ms[1, MR:] = split(m_t)

    KR = R // 2
    half = BY // 2
    hb = by - 1
    KY, KZ, KC = NBY * SLOT, NBZ * BY, NBZ * NBY

    def more_tables():
        gye, gze = gye_v[...], gze_v[...]
        ty[0] = jnp.broadcast_to(gye[:, 0:1] / gye[0:1, 0:1], (BY, NX))
        ty[1] = jnp.broadcast_to(gye[:, BY - 1 : BY] / gye[BY - 1 : BY, BY - 1 : BY], (BY, NX))
        last = R - BY
        tz[0] = jnp.broadcast_to(gze[:, 0:1] / gze[0:1, 0:1], (BZ, NX))
        tz[1] = jnp.broadcast_to(gze[:, last : last + 1] / gze[BZ - 1 : BZ, last : last + 1], (BZ, NX))

        i, j = rows_of((KR, KR)), cols_of((KR, KR))
        tiled = jnp.concatenate([gye[:, 0:KR]] * (KR // BY), axis=0)
        bdy[0], bdy[1] = split(jnp.where(halved(i, by) == halved(j, by), tiled, 0.0))
        k, c = rows_of((BZ * NBZ, KR)), cols_of((BZ * NBZ, KR))
        gzh = exact(gz_v[pl.ds(pl.multiple_of(b * BZ, BZ), BZ), :], onehot(k == b * BZ + halved(c, hb)))
        spread = exact(onehot(halved(rows_of((KR, BZ)), hb) == cols_of((KR, BZ))), gzh)
        kz[0], kz[1] = split(jnp.where((i & (half - 1)) == (j & (half - 1)), spread, 0.0))

        wl, wr = coarse(gy_v[...], BY, NBY)
        w = jnp.where(side == 0, wl, wr)
        wide = exact(w, onehot(rows_of((NBY, KY)) == over_slot(cols_of((NBY, KY)))))
        full = exact(onehot(over_slot(rows_of((KY, NBY))) == cols_of((KY, NBY))), wide)
        i, j = rows_of((KY, KY)), cols_of((KY, KY))
        ii = i - SLOT * over_slot(i)
        kw[0], kw[1] = split(jnp.where((ii == j - SLOT * over_slot(j)) & (ii < BZ), full, 0.0))
        i, j = rows_of((2 * NBY, KY)), cols_of((2 * NBY, KY))
        kind = jnp.where(i >= NBY, 1, 0)
        pick = exact(onehot(rows_of((2 * NBY, NBY)) - NBY * jnp.where(rows_of((2 * NBY, NBY)) >= NBY, 1, 0)
                            == cols_of((2 * NBY, NBY))), wide)
        kwc[0], kwc[1] = split(jnp.where(j - SLOT * over_slot(j) == BZ + kind, pick, 0.0))

        wl, wr = coarse(gz_v[...], BZ, NBZ)
        i, j = rows_of((KZ, KZ)), cols_of((KZ, KZ))
        same = (i & (BY - 1)) == (j & (BY - 1))
        down = onehot(halved(rows_of((KZ, NBZ)), by) == cols_of((KZ, NBZ)))
        across = onehot(rows_of((NBZ, KZ)) == halved(cols_of((NBZ, KZ)), by))
        kzl[0], kzl[1] = split(jnp.where(same, exact(down, exact(wl, across)), 0.0))
        kzr[0], kzr[1] = split(jnp.where(same, exact(down, exact(wr, across)), 0.0))
        mine = onehot(cols_of((NBZ, NBZ)) == b)
        nb = NBY.bit_length() - 1
        across = onehot(rows_of((NBZ, KC)) == halved(cols_of((NBZ, KC)), nb))
        row_l = exact(exact(mine, wl), across)[0:1]
        row_r = exact(exact(mine, wr), across)[0:1]
        i, j = rows_of((KY, KC)), cols_of((KY, KC))
        ii = i - SLOT * over_slot(i)
        value = jnp.where(ii == BZ, row_l, jnp.where(ii == BZ + 1, row_r, 0.0))
        kcs[0], kcs[1] = split(jnp.where(over_slot(i) == (j & (NBY - 1)), value, 0.0))

    crecv[:, b] = jnp.zeros((STEPS, NBY, LANES), F32)
    for load in loads[4:]:
        load.wait()
    for n in range(turns):
        gxs[0, n], gxs[1, n] = split(gx_v[n])
    loads[2].wait()
    loads[3].wait()

    def chunk(t):
        return pl.ds(pl.multiple_of(t * CW, CW), CW)

    def lanes(t):
        return pl.ds(pl.multiple_of(t * LANES, LANES), LANES)

    def pair(ref, *at):
        return ref[(0, *at)], ref[(1, *at)]

    def settle(ref, sem):
        pltpu.make_async_copy(ref, ref, sem).wait()

    def along_x(source, target, rows, extra):
        first, last = [], []
        for n in range(turns):
            at = slice(n * CW, (n + 1) * CW)
            part = product((source[0, rows, at], source[1, rows, at]), pair(gxs, n))
            target[rows, at] = part + extra(at)
            first.append(part[:, 0:1])
            last.append(part[:, CW - 1 : CW])
        ups, downs = [None] * turns, [None] * turns
        carry = last[0]
        for n in range(1, turns):
            edge = edge_v[n - 1, 7:8, n * CW : (n + 1) * CW] / edge_v[n - 1, 7:8, n * CW - 1 : n * CW]
            ups[n] = (carry, edge)
            carry = last[n] + carry * edge[:, CW - 1 : CW]
        carry = first[turns - 1]
        for n in range(turns - 2, -1, -1):
            at = (n + 1) * CW
            edge = edge_v[n, 8:9, n * CW : at] / edge_v[n, 8:9, at : at + 1]
            downs[n] = (carry, edge)
            carry = first[n] + carry * edge[:, 0:1]
        for n in range(turns):
            at = slice(n * CW, (n + 1) * CW)
            terms = [p[0] * p[1] for p in (ups[n], downs[n]) if p is not None]
            if terms:
                target[rows, at] += sum(terms[1:], terms[0])

    def prepare(field, at):
        psi = field * (8.0 - 2.0 * field * field - 4.0 * oth_v[at])
        phs[(0, *at)], phs[(1, *at)] = split(field)
        pss[(0, *at)], pss[(1, *at)] = split(psi)

    def prepare_rows(z, _):
        at = (pl.ds(pl.multiple_of(z * BY, BY), BY), slice(None))
        prepare(phi_v[at], at)
        return _

    lax.fori_loop(0, BZ, prepare_rows, 0)

    ends = (
        (loc, loc_h),
        (phi_v.at[0:BZ], yl_h), (phi_v.at[BZ : 2 * BZ], yr_h),
        (phi_v.at[2 * BZ : 2 * BZ + BY], zl_h), (phi_v.at[2 * BZ + BY : 2 * BZ + 2 * BY], zr_h),
        (ty.at[0], tyl_h), (ty.at[1], tyr_h), (tz.at[0], tzl_h), (tz.at[1], tzr_h),
    )
    ends = [pltpu.make_async_copy(x, y, own_sem.at[n]) for n, (x, y) in enumerate(ends)]

    def step(s, carry):
        def reduce(t, _):
            at = chunk(t)
            both = product(pair(ms), (phs[0, :, at], phs[1, :, at]))
            first = product((ms[0, 0:MR], ms[1, 0:MR]), (pss[0, :, at], pss[1, :, at]))
            acs[0, :, at], acs[1, :, at] = split(first - 2.0 * both[MR:])
            bb[:, at] = -2.0 * both[0:MR]
            return _

        lax.fori_loop(0, turns, reduce, 0)
        along_x(acs, red.at[s], slice(0, MR), lambda at: bb[:, at])

        @pl.when(s == 0)
        def _():
            pl.semaphore_wait(barrier, NBY + NBZ - 2)

        def send_y(k, _):
            to = (a + k) % NBY
            pltpu.make_async_remote_copy(
                src_ref=red.at[s, pl.ds(pl.multiple_of((to % 2) * SLOT, 8), SLOT), lanes(to // 2)],
                dst_ref=yrecv.at[s, a],
                send_sem=send_sem.at[s, 0], recv_sem=recv_sem.at[s, 0],
                device_id=(to, b), device_id_type=MESH,
            ).start()
            return _

        def send_z(k, _):
            to = (b + k) % NBZ
            pltpu.make_async_remote_copy(
                src_ref=red.at[s, pl.ds(YM, 2 * BY), lanes(to)],
                dst_ref=zrecv.at[s, b],
                send_sem=send_sem.at[s, 1], recv_sem=recv_sem.at[s, 1],
                device_id=(a, to), device_id_type=MESH,
            ).start()
            return _

        lax.fori_loop(1, NBY, send_y, 0)
        lax.fori_loop(1, NBZ, send_z, 0)
        yrecv[s, a] = red[s, pl.ds(pl.multiple_of(side * SLOT, 8), SLOT), lanes(piece)]
        zrecv[s, b] = red[s, pl.ds(YM, 2 * BY), lanes(b)]

        def local(t, _):
            at = chunk(t)
            v, w = [], []
            for h in range(2):
                def rows(ref, q):
                    part = ref[q, :, at].reshape(BZ, 2, half, CW)
                    return part[:, h].reshape(KR, CW)

                v.append(product(pair(kz), (rows(phs, 0), rows(phs, 1))).reshape(BZ, half, CW))
                w.append(product(pair(kz), (rows(pss, 0), rows(pss, 1))).reshape(BZ, half, CW))
            v = jnp.concatenate(v, axis=1).reshape(R, CW)
            w = jnp.concatenate(w, axis=1).reshape(R, CW)
            field = phi_v[:, at]
            g = split(w - 2.0 * field)
            vs = split(v)
            for h in range(2):
                at_h = slice(h * KR, (h + 1) * KR)
                first = product(pair(bdy), (g[0][at_h], g[1][at_h]))
                second = product(pair(bdy), (vs[0][at_h], vs[1][at_h]))
                hs[0, at_h, at], hs[1, at_h, at] = split(first - 2.0 * v[at_h])
                loc[at_h, at] = field[at_h] - 2.0 * second
            return _

        early = min(1, turns)

        @pl.when(s == 0)
        def _():
            more_tables()
            for end in ends[5:]:
                end.start()

        @pl.when(s > 0)
        def _():
            lax.fori_loop(0, turns, local, 0)

        settle(yrecv.at[s, pl.ds(0, NBY - 1)], recv_sem.at[s, 0])
        ys = split(yrecv[s].reshape(KY, LANES))
        csend[s] = product(pair(kwc), ys)

        def send_c(k, _):
            to = (b + k) % NBZ
            which = 1 - (to - b + NBZ) // NBZ
            pltpu.make_async_remote_copy(
                src_ref=csend.at[s, pl.ds(pl.multiple_of(which * NBY, NBY), NBY)],
                dst_ref=crecv.at[s, b],
                send_sem=send_sem.at[s, 2], recv_sem=recv_sem.at[s, 2],
                device_id=(a, to), device_id_type=MESH,
            ).start()
            return _

        lax.fori_loop(1, NBZ, send_c, 0)
        ymain[...] = product(pair(kw), ys)

        settle(zrecv.at[s, pl.ds(0, NBZ - 1)], recv_sem.at[s, 1])
        for n, matrix in enumerate((kzl, kzr)):
            part = zrecv[s, :, n * BY : (n + 1) * BY].reshape(KZ, LANES)
            zback[s, :, n * BY : (n + 1) * BY] = product(pair(matrix), split(part)).reshape(NBZ, BY, LANES)

        def return_z(k, _):
            to = (b + k) % NBZ
            pltpu.make_async_remote_copy(
                src_ref=zback.at[s, to],
                dst_ref=cmat.at[s, pl.ds(YM, 2 * BY), lanes(b)],
                send_sem=send_sem.at[s, 3], recv_sem=recv_sem.at[s, 3],
                device_id=(a, to), device_id_type=MESH,
            ).start()
            return _

        lax.fori_loop(1, NBZ, return_z, 0)
        cmat[s, pl.ds(YM, 2 * BY), lanes(b)] = zback[s, b]

        @pl.when(s == 0)
        def _():
            lax.fori_loop(0, early, local, 0)

        settle(crecv.at[s, pl.ds(0, NBZ - 1)], recv_sem.at[s, 2])
        corners = product(pair(kcs), split(crecv[s].reshape(KC, LANES)))
        yback[s] = (ymain[...] + corners).reshape(NBY, SLOT, LANES)

        def return_y(k, _):
            to = (a + k) % NBY
            pltpu.make_async_remote_copy(
                src_ref=yback.at[s, to],
                dst_ref=cmat.at[s, pl.ds(pl.multiple_of(side * SLOT, 8), SLOT), lanes(piece)],
                send_sem=send_sem.at[s, 4], recv_sem=recv_sem.at[s, 4],
                device_id=(to, b), device_id_type=MESH,
            ).start()
            return _

        lax.fori_loop(1, NBY, return_y, 0)
        cmat[s, pl.ds(pl.multiple_of(side * SLOT, 8), SLOT), lanes(piece)] = yback[s, a]

        @pl.when(s == 0)
        def _():
            lax.fori_loop(early, turns, local, 0)

        def local_x(t, _):
            rows = pl.ds(pl.multiple_of(t * 128, 128), 128)
            along_x(hs, loc, rows, lambda at: loc[rows, at])
            return _

        lax.fori_loop(0, R // 128, local_x, 0)

        @pl.when(s == STEPS - 1)
        def _():
            ends[0].start()

        settle(zrecv.at[s, pl.ds(0, NBZ - 1)], recv_sem.at[s, 3])
        settle(yrecv.at[s, pl.ds(0, NBY - 1)], recv_sem.at[s, 4])

        @pl.when(s < STEPS - 1)
        def _():
            def add(c, _):
                at = lanes(c)
                sums = [cmat[s, r : r + n, at] for r, n in parts(BY, BZ)]
                expand(BY, BZ, sums, ty, tz, lambda rows: loc[rows, at], lambda rows, v: put(rows, at, v))
                return _

            def put(rows, at, value):
                phi_v[rows, at] = value
                prepare(value, (rows, at))

            lax.fori_loop(0, NX // LANES, add, 0)

        @pl.when(s == STEPS - 1)
        def _():
            def gather(c, _):
                at = lanes(c)
                sums = [cmat[s, r : r + n, at] for r, n in parts(BY, BZ)]
                zl, zr = fold(sums, ty)
                phi_v[0:BZ, at], phi_v[BZ : 2 * BZ, at] = sums[0], sums[3]
                phi_v[2 * BZ : 2 * BZ + BY, at], phi_v[2 * BZ + BY : 2 * BZ + 2 * BY, at] = zl, zr
                return _

            lax.fori_loop(0, NX // LANES, gather, 0)
            for end in ends[1:5]:
                end.start()

        for n in (0, 4):
            settle(yrecv.at[s, pl.ds(0, NBY - 1)], send_sem.at[s, n])
        for n in (1, 3):
            settle(zrecv.at[s, pl.ds(0, NBZ - 1)], send_sem.at[s, n])
        settle(crecv.at[s, pl.ds(0, NBZ - 1)], send_sem.at[s, 2])
        return carry

    lax.fori_loop(0, STEPS, step, 0)
    for end in ends:
        end.wait()


def parts(BY, BZ):
    return (0, BZ), (BZ, 1), (BZ + 1, 1), (SLOT, BZ), (SLOT + BZ, 1), (SLOT + BZ + 1, 1), \
        (2 * SLOT, BY), (2 * SLOT + BY, BY)


def fold(sums, ty):
    _, cll, clr, _, crl, crr, zl, zr = sums
    left, right = ty[0, :, 0:LANES], ty[1, :, 0:LANES]
    return zl + left * cll + right * crl, zr + left * clr + right * crr


def expand(BY, BZ, sums, ty, tz, get, put):
    yl, yr = sums[0], sums[3]
    zl, zr = fold(sums, ty)
    left, right = ty[0, :, 0:LANES], ty[1, :, 0:LANES]
    for z in range(BZ):
        rows = slice(z * BY, (z + 1) * BY)
        ends = left * yl[z : z + 1] + right * yr[z : z + 1]
        put(rows, get(rows) + ends + tz[0, z : z + 1, 0:LANES] * zl + tz[1, z : z + 1, 0:LANES] * zr)


def body(NBY, NBZ, phase_field, others, cond_x, cond_y, cond_z, inverse_x, inverse_y, inverse_z):
    BZ, BY, NX = phase_field.shape
    R = BY * BZ
    MR = 2 * SLOT + 2 * BY
    KR, KY, KZ, KC = R // 2, NBY * SLOT, NBZ * BY, NBZ * NBY
    vmem = pltpu.VMEM
    CW, turns = 256, NX // 256
    call = pl.pallas_call(
        functools.partial(kernel, NBY, NBZ, BY, BZ, NX),
        out_shape=[
            jax.ShapeDtypeStruct((n, NX), F32) for n in (R, BZ, BZ, BY, BY, BY, BY, BZ, BZ)
        ],
        in_specs=[pl.BlockSpec(memory_space=pl.ANY)] * 5,
        out_specs=[pl.BlockSpec(memory_space=pl.ANY)] * 9,
        scratch_shapes=[
            vmem((R, NX), F32), vmem((R, NX), F32), vmem((turns, CW, CW), F32),
            vmem((max(turns - 1, 1), 16, NX), F32),
            vmem((BY * NBY, BY * NBY), F32), vmem((BZ * NBZ, BZ * NBZ), F32),
            vmem((BY, R), F32), vmem((BZ, R), F32),
            vmem((2, turns, CW, CW), BF16), vmem((2, 2 * MR, R), BF16), vmem((2, KR, KR), BF16),
            vmem((2, KR, KR), BF16), vmem((2, BY, NX), F32), vmem((2, BZ, NX), F32),
            vmem((2, KY, KY), BF16),
            vmem((2, 2 * NBY, KY), BF16), vmem((2, KY, KC), BF16), vmem((2, KZ, KZ), BF16),
            vmem((2, KZ, KZ), BF16),
            vmem((2, R, NX), BF16), vmem((2, R, NX), BF16), vmem((2, R, NX), BF16),
            vmem((2, MR, NX), BF16), vmem((MR, NX), F32), vmem((R, NX), F32),
            vmem((STEPS, MR, NX), F32), vmem((STEPS, NBY, SLOT, LANES), F32),
            vmem((STEPS, NBZ, 2 * BY, LANES), F32), vmem((STEPS, NBZ, NBY, LANES), F32),
            vmem((STEPS, 2 * NBY, LANES), F32), vmem((STEPS, NBY, SLOT, LANES), F32),
            vmem((STEPS, NBZ, 2 * BY, LANES), F32), vmem((KY, LANES), F32),
            vmem((STEPS, MR, NX), F32),
            pltpu.SemaphoreType.DMA((2 * turns + 3,)), pltpu.SemaphoreType.DMA((9,)),
            pltpu.SemaphoreType.DMA((STEPS, 5)), pltpu.SemaphoreType.DMA((STEPS, 5)),
        ],
        compiler_params=pltpu.CompilerParams(
            collective_id=0, has_side_effects=True, vmem_limit_bytes=56 << 20
        ),
        name="adi",
    )
    loc, yl, yr, zl, zr, tyl, tyr, tzl, tzr = call(
        phase_field.reshape(R, NX), others.reshape(R, NX), inverse_x, inverse_y, inverse_z
    )
    along_y = tyl[None] * yl[:, None] + tyr[None] * yr[:, None]
    along_z = tzl[:, None] * zl[None] + tzr[:, None] * zr[None]
    return loc.reshape(BZ, BY, NX) + along_y + along_z


def solution(mesh):
    placed = (P("gz", "gy", None), P("gz", "gy", None), P(), P(), P(), P(), P(), P())
    return jax.shard_map(
        functools.partial(body, mesh.shape["gy"], mesh.shape["gz"]),
        mesh=mesh, in_specs=placed, out_specs=P("gz", "gy", None), check_vma=False,
    )
```

```python
import functools

import jax
import jax.numpy as jnp
from jax import lax
from jax.experimental import pallas as pl
from jax.experimental.pallas import tpu as pltpu
from jax.sharding import PartitionSpec as P

STEPS = 2
LANES = 128
F32 = jnp.float32
BF16 = jnp.bfloat16
MESH = pl.DeviceIdType.MESH


def exact(a, b):
    return jnp.dot(a, b, precision=lax.Precision.HIGHEST, preferred_element_type=F32)


def split(x):
    high = x.astype(BF16)
    return high, (x - high.astype(F32)).astype(BF16)


def product(a, b):
    dot = functools.partial(jnp.dot, preferred_element_type=F32)
    return dot(a[0], b[0]) + (dot(a[1], b[0]) + dot(a[0], b[1]))


def rows_of(shape):
    return lax.broadcasted_iota(jnp.int32, shape, 0)


def cols_of(shape):
    return lax.broadcasted_iota(jnp.int32, shape, 1)


def halved(i, bits):
    return lax.shift_right_logical(i, jnp.full_like(i, bits))


def onehot(mask):
    return jnp.where(mask, 1.0, 0.0).astype(F32)


def coarse(inverse, size, blocks):
    width = size * blocks
    at = cols_of((blocks, width)) - rows_of((blocks, width)) * size
    first_rows, last_rows = exact(onehot(at == 0), inverse), exact(onehot(at == size - 1), inverse)
    at = rows_of((width, blocks)) - cols_of((width, blocks)) * size
    first, last = onehot(at == 0), onehot(at == size - 1)
    i, j = rows_of((blocks, blocks)), cols_of((blocks, blocks))
    last_last = jnp.sum(jnp.where(i == j, exact(last_rows, last), 0.0), axis=0, keepdims=True)
    first_first = jnp.sum(jnp.where(i == j, exact(first_rows, first), 0.0), axis=0, keepdims=True)
    left = jnp.where(j < i, exact(first_rows, last) / last_last, 0.0)
    right = jnp.where(j > i, exact(last_rows, first) / first_first, 0.0)
    return left, right


def kernel(
    NBY, NBZ, BY, BZ, NX,
    phi_h, oth_h, gx_h, gy_h, gz_h, loc, yl_o, yr_o, zl_o, zr_o, tyl, tyr, tzl, tzr,
    phi_v, oth_v, gx_v, edge_v, gy_v, gym_v, gz_v, gye_v, gze_v,
    gxs, ms, kz, bdy, kw, cyw, czw, kzl, kzr,
    phs, pss, hs, acs, bb,
    red, yrecv, zrecv, cy, csend, cz, corn, yback, zback, cmat,
    load_sem, send_sem, recv_sem,
):
    a, b = lax.axis_index("gy"), lax.axis_index("gz")
    piece, side = a // 2, a % 2
    ty, tz = (tyl, tyr), (tzl, tzr)
    R = BY * BZ
    by, bz = BY.bit_length() - 1, BZ.bit_length() - 1
    YM = 2 * BZ
    CM = YM + 2 * BY
    MR = CM + 16
    CW = 256
    turns = NX // CW

    barrier = pltpu.get_barrier_semaphore()

    def greet_y(k, _):
        pl.semaphore_signal(barrier, inc=1, device_id=((a + k) % NBY, b), device_id_type=MESH)
        return _

    def greet_z(k, _):
        pl.semaphore_signal(barrier, inc=1, device_id=(a, (b + k) % NBZ), device_id_type=MESH)
        return _

    lax.fori_loop(1, NBY, greet_y, 0)
    lax.fori_loop(1, NBZ, greet_z, 0)

    mine = pl.ds(pl.multiple_of(a * BY, BY), BY)
    pairs = [(gy_h.at[mine], gym_v), (gz_h, gz_v), (phi_h, phi_v), (oth_h, oth_v)]
    for n in range(turns):
        pairs.append((gx_h.at[pl.ds(n * CW, CW), pl.ds(n * CW, CW)], gx_v.at[n]))
    for n in range(turns - 1):
        pairs.append((gx_h.at[pl.ds((n + 1) * CW - 8, 16)], edge_v.at[n]))
    pairs.append((gy_h, gy_v))
    loads = [pltpu.make_async_copy(s, d, load_sem.at[i]) for i, (s, d) in enumerate(pairs)]
    for load in loads:
        load.start()
    loads[0].wait()
    loads[1].wait()

    wide = min(LANES, BY * NBY)
    start = (a * BY // wide) * wide
    k, c = rows_of((wide, R)), cols_of((wide, R))
    gye = exact(
        gym_v[:, pl.ds(pl.multiple_of(start, wide), wide)],
        onehot(k == a * BY - start + (c & (BY - 1))),
    )
    k, c = rows_of((BZ * NBZ, R)), cols_of((BZ * NBZ, R))
    gze = exact(gz_v[pl.ds(pl.multiple_of(b * BZ, BZ), BZ), :], onehot(k == b * BZ + halved(c, by)))
    gye_v[...], gze_v[...] = gye, gze
    oz = onehot(rows_of((BZ, R)) == halved(cols_of((BZ, R)), by))
    oy = onehot(rows_of((BY, R)) == (cols_of((BY, R)) & (BY - 1)))
    yl, yf = gye[BY - 1 : BY], gye[0:1]
    zl, zf = gze[BZ - 1 : BZ], gze[0:1]

    def corner(first, second):
        i = rows_of((8, R))
        return jnp.where(i == 0, first, jnp.where(i == 1, second, 0.0))

    m_s = jnp.concatenate(
        [gze * yl, gze * yf, gye * zl, gye * zf, corner(zl * yl, zf * yl), corner(zl * yf, zf * yf)], axis=0
    )
    m_t = jnp.concatenate([oz * yl, oz * yf, oy * zl, oy * zf, jnp.zeros((16, R), F32)], axis=0)
    ms[0, 0:MR], ms[1, 0:MR] = split(m_s)
    ms[0, MR:], ms[1, MR:] = split(m_t)

    KR = R // 2
    half = BY // 2
    hb = by - 1
    KY, KZ = NBY * BZ, NBZ * BY

    def more_tables():
        loads[-1].wait()
        gye, gze = gye_v[...], gze_v[...]
        tyl[...] = jnp.broadcast_to(gye[:, 0:1] / gye[0:1, 0:1], (BY, NX))
        tyr[...] = jnp.broadcast_to(gye[:, BY - 1 : BY] / gye[BY - 1 : BY, BY - 1 : BY], (BY, NX))
        last = R - BY
        tzl[...] = jnp.broadcast_to(gze[:, 0:1] / gze[0:1, 0:1], (BZ, NX))
        tzr[...] = jnp.broadcast_to(gze[:, last : last + 1] / gze[BZ - 1 : BZ, last : last + 1], (BZ, NX))

        i, j = rows_of((KR, KR)), cols_of((KR, KR))
        tiled = jnp.concatenate([gye[:, 0:KR]] * (KR // BY), axis=0)
        bdy[0], bdy[1] = split(jnp.where(halved(i, by) == halved(j, by), tiled, 0.0))
        k, c = rows_of((BZ * NBZ, KR)), cols_of((BZ * NBZ, KR))
        gzh = exact(gz_v[pl.ds(pl.multiple_of(b * BZ, BZ), BZ), :], onehot(k == b * BZ + halved(c, hb)))
        spread = exact(onehot(halved(rows_of((KR, BZ)), hb) == cols_of((KR, BZ))), gzh)
        kz[0], kz[1] = split(jnp.where((i & (half - 1)) == (j & (half - 1)), spread, 0.0))

        wl, wr = coarse(gy_v[...], BY, NBY)
        w = jnp.where(side == 0, wl, wr)
        i, j = rows_of((KY, KY)), cols_of((KY, KY))
        same = (i & (BZ - 1)) == (j & (BZ - 1))
        down = onehot(halved(rows_of((KY, NBY)), bz) == cols_of((KY, NBY)))
        across = onehot(rows_of((NBY, KY)) == halved(cols_of((NBY, KY)), bz))
        kw[0], kw[1] = split(jnp.where(same, exact(down, exact(w, across)), 0.0))
        mine = onehot(cols_of((16, NBY)) == a)
        across = onehot(rows_of((NBY, 8 * NBY)) == halved(cols_of((NBY, 8 * NBY)), 3))
        i, j = rows_of((16, 8 * NBY)), cols_of((16, 8 * NBY))
        row_l, row_r = exact(exact(mine, wl), across), exact(exact(mine, wr), across)
        value = jnp.where((i & 7) == 0, row_l, jnp.where((i & 7) == 1, row_r, 0.0))
        cyw[0], cyw[1] = split(jnp.where((j & 7) == halved(i, 3), value, 0.0))

        wl, wr = coarse(gz_v[...], BZ, NBZ)
        i, j = rows_of((KZ, KZ)), cols_of((KZ, KZ))
        same = (i & (BY - 1)) == (j & (BY - 1))
        down = onehot(halved(rows_of((KZ, NBZ)), by) == cols_of((KZ, NBZ)))
        across = onehot(rows_of((NBZ, KZ)) == halved(cols_of((NBZ, KZ)), by))
        kzl[0], kzl[1] = split(jnp.where(same, exact(down, exact(wl, across)), 0.0))
        kzr[0], kzr[1] = split(jnp.where(same, exact(down, exact(wr, across)), 0.0))
        mine = onehot(cols_of((8, NBZ)) == b)
        across = onehot(rows_of((NBZ, 8 * NBZ)) == halved(cols_of((NBZ, 8 * NBZ)), 3))
        i, j = rows_of((8, 8 * NBZ)), cols_of((8, 8 * NBZ))
        row_l, row_r = exact(exact(mine, wl), across), exact(exact(mine, wr), across)
        value = jnp.where(i < 2, row_l, jnp.where(i < 4, row_r, 0.0))
        czw[0], czw[1] = split(jnp.where((j & 7) == (i & 1), value, 0.0))

    cy[:, :, 2:8] = jnp.zeros((STEPS, NBY, 6, NX), F32)
    cz[:, :, 2:8] = jnp.zeros((STEPS, NBZ, 6, NX), F32)
    cy[:, a, 0:2] = jnp.zeros((STEPS, 2, NX), F32)
    cz[:, b, 0:2] = jnp.zeros((STEPS, 2, NX), F32)
    for load in loads[4:-1]:
        load.wait()
    for n in range(turns):
        gxs[0, n], gxs[1, n] = split(gx_v[n])
    loads[2].wait()
    loads[3].wait()

    def chunk(t):
        return pl.ds(pl.multiple_of(t * CW, CW), CW)

    def lanes(t):
        return pl.ds(pl.multiple_of(t * LANES, LANES), LANES)

    def pair(ref, *at):
        return ref[(0, *at)], ref[(1, *at)]

    def settle(ref, sem):
        pltpu.make_async_copy(ref, ref, sem).wait()

    def along_x(source, target, rows, extra):
        first, last = [], []
        for n in range(turns):
            at = slice(n * CW, (n + 1) * CW)
            part = product((source[0, rows, at], source[1, rows, at]), pair(gxs, n))
            target[rows, at] = part + extra(at)
            first.append(part[:, 0:1])
            last.append(part[:, CW - 1 : CW])
        ups, downs = [None] * turns, [None] * turns
        carry = last[0]
        for n in range(1, turns):
            edge = edge_v[n - 1, 7:8, n * CW : (n + 1) * CW] / edge_v[n - 1, 7:8, n * CW - 1 : n * CW]
            ups[n] = (carry, edge)
            carry = last[n] + carry * edge[:, CW - 1 : CW]
        carry = first[turns - 1]
        for n in range(turns - 2, -1, -1):
            at = (n + 1) * CW
            edge = edge_v[n, 8:9, n * CW : at] / edge_v[n, 8:9, at : at + 1]
            downs[n] = (carry, edge)
            carry = first[n] + carry * edge[:, 0:1]
        for n in range(turns):
            at = slice(n * CW, (n + 1) * CW)
            terms = [p[0] * p[1] for p in (ups[n], downs[n]) if p is not None]
            if terms:
                target[rows, at] += sum(terms[1:], terms[0])

    def prepare(field, at):
        psi = field * (8.0 - 2.0 * field * field - 4.0 * oth_v[at])
        phs[(0, *at)], phs[(1, *at)] = split(field)
        pss[(0, *at)], pss[(1, *at)] = split(psi)

    def prepare_rows(z, _):
        at = (pl.ds(pl.multiple_of(z * BY, BY), BY), slice(None))
        prepare(phi_v[at], at)
        return _

    lax.fori_loop(0, BZ, prepare_rows, 0)

    def step(s, carry):
        def reduce(t, _):
            at = chunk(t)
            both = product(pair(ms), (phs[0, :, at], phs[1, :, at]))
            first = product((ms[0, 0:MR], ms[1, 0:MR]), (pss[0, :, at], pss[1, :, at]))
            acs[0, :, at], acs[1, :, at] = split(first - 2.0 * both[MR:])
            bb[:, at] = -2.0 * both[0:MR]
            return _

        lax.fori_loop(0, turns, reduce, 0)
        along_x(acs, red.at[s], slice(0, MR), lambda at: bb[:, at])

        @pl.when(s == 0)
        def _():
            pl.semaphore_wait(barrier, NBY + NBZ - 2)

        def send_c(k, _):
            to = (a + k) % NBY
            which = 1 - (to - a + NBY) // NBY
            pltpu.make_async_remote_copy(
                src_ref=red.at[s, pl.ds(pl.multiple_of(CM + 8 * which, 8), 2)],
                dst_ref=cy.at[s, a, pl.ds(0, 2)],
                send_sem=send_sem.at[s, 2], recv_sem=recv_sem.at[s, 2],
                device_id=(to, b), device_id_type=MESH,
            ).start()
            return _

        def send_y(k, _):
            to = (a + k) % NBY
            pltpu.make_async_remote_copy(
                src_ref=red.at[s, pl.ds(pl.multiple_of((to % 2) * BZ, 8), BZ), lanes(to // 2)],
                dst_ref=yrecv.at[s, a],
                send_sem=send_sem.at[s, 0], recv_sem=recv_sem.at[s, 0],
                device_id=(to, b), device_id_type=MESH,
            ).start()
            return _

        def send_z(k, _):
            to = (b + k) % NBZ
            pltpu.make_async_remote_copy(
                src_ref=red.at[s, pl.ds(YM, 2 * BY), lanes(to)],
                dst_ref=zrecv.at[s, b],
                send_sem=send_sem.at[s, 1], recv_sem=recv_sem.at[s, 1],
                device_id=(a, to), device_id_type=MESH,
            ).start()
            return _

        lax.fori_loop(1, NBY, send_c, 0)
        lax.fori_loop(1, NBY, send_y, 0)
        lax.fori_loop(1, NBZ, send_z, 0)
        yrecv[s, a] = red[s, pl.ds(pl.multiple_of(side * BZ, 8), BZ), lanes(piece)]
        zrecv[s, b] = red[s, pl.ds(YM, 2 * BY), lanes(b)]

        def local(t, _):
            at = chunk(t)
            v, w = [], []
            for h in range(2):
                def rows(ref, q):
                    part = ref[q, :, at].reshape(BZ, 2, half, CW)
                    return part[:, h].reshape(KR, CW)

                v.append(product(pair(kz), (rows(phs, 0), rows(phs, 1))).reshape(BZ, half, CW))
                w.append(product(pair(kz), (rows(pss, 0), rows(pss, 1))).reshape(BZ, half, CW))
            v = jnp.concatenate(v, axis=1).reshape(R, CW)
            w = jnp.concatenate(w, axis=1).reshape(R, CW)
            field = phi_v[:, at]
            g = split(w - 2.0 * field)
            vs = split(v)
            for h in range(2):
                at_h = slice(h * KR, (h + 1) * KR)
                first = product(pair(bdy), (g[0][at_h], g[1][at_h]))
                second = product(pair(bdy), (vs[0][at_h], vs[1][at_h]))
                hs[0, at_h, at], hs[1, at_h, at] = split(first - 2.0 * v[at_h])
                loc[at_h, at] = field[at_h] - 2.0 * second
            return _

        early = min(1, turns)

        @pl.when(s == 0)
        def _():
            more_tables()

        @pl.when(s > 0)
        def _():
            lax.fori_loop(0, turns, local, 0)

        @pl.when(s == 0)
        def _():
            lax.fori_loop(0, early, local, 0)

        settle(cy.at[s, pl.ds(0, NBY - 1), pl.ds(0, 2)], recv_sem.at[s, 2])
        csend[s] = product(pair(cyw), split(cy[s].reshape(8 * NBY, NX))).reshape(2, 8, NX)

        def pass_c(k, _):
            to = (b + k) % NBZ
            which = 1 - (to - b + NBZ) // NBZ
            pltpu.make_async_remote_copy(
                src_ref=csend.at[s, which, pl.ds(0, 2)],
                dst_ref=cz.at[s, b, pl.ds(0, 2)],
                send_sem=send_sem.at[s, 5], recv_sem=recv_sem.at[s, 5],
                device_id=(a, to), device_id_type=MESH,
            ).start()
            return _

        lax.fori_loop(1, NBZ, pass_c, 0)

        settle(yrecv.at[s, pl.ds(0, NBY - 1)], recv_sem.at[s, 0])
        yback[s] = product(pair(kw), split(yrecv[s].reshape(KY, LANES))).reshape(NBY, BZ, LANES)

        def return_y(k, _):
            to = (a + k) % NBY
            pltpu.make_async_remote_copy(
                src_ref=yback.at[s, to],
                dst_ref=cmat.at[s, pl.ds(pl.multiple_of(side * BZ, 8), BZ), lanes(piece)],
                send_sem=send_sem.at[s, 4], recv_sem=recv_sem.at[s, 4],
                device_id=(to, b), device_id_type=MESH,
            ).start()
            return _

        lax.fori_loop(1, NBY, return_y, 0)
        cmat[s, pl.ds(pl.multiple_of(side * BZ, 8), BZ), lanes(piece)] = yback[s, a]

        settle(zrecv.at[s, pl.ds(0, NBZ - 1)], recv_sem.at[s, 1])
        for n, matrix in enumerate((kzl, kzr)):
            part = zrecv[s, :, n * BY : (n + 1) * BY].reshape(KZ, LANES)
            zback[s, :, n * BY : (n + 1) * BY] = product(pair(matrix), split(part)).reshape(NBZ, BY, LANES)

        def return_z(k, _):
            to = (b + k) % NBZ
            pltpu.make_async_remote_copy(
                src_ref=zback.at[s, to],
                dst_ref=cmat.at[s, pl.ds(YM, 2 * BY), lanes(b)],
                send_sem=send_sem.at[s, 3], recv_sem=recv_sem.at[s, 3],
                device_id=(a, to), device_id_type=MESH,
            ).start()
            return _

        lax.fori_loop(1, NBZ, return_z, 0)
        cmat[s, pl.ds(YM, 2 * BY), lanes(b)] = zback[s, b]

        @pl.when(s == 0)
        def _():
            lax.fori_loop(early, turns, local, 0)

        def local_x(t, _):
            rows = pl.ds(pl.multiple_of(t * 128, 128), 128)
            along_x(hs, loc, rows, lambda at: loc[rows, at])
            return _

        lax.fori_loop(0, R // 128, local_x, 0)

        settle(cz.at[s, pl.ds(0, NBZ - 1), pl.ds(0, 2)], recv_sem.at[s, 5])
        corn[...] = product(pair(czw), split(cz[s].reshape(8 * NBZ, NX)))
        settle(yrecv.at[s, pl.ds(0, NBY - 1)], recv_sem.at[s, 4])
        settle(zrecv.at[s, pl.ds(0, NBZ - 1)], recv_sem.at[s, 3])

        @pl.when(s < STEPS - 1)
        def _():
            def add(c, _):
                at = lanes(c)
                sums = [cmat[s, r : r + n, at] for r, n in parts(BY, BZ)] + [corn[:, at]]
                expand(BY, BZ, sums, ty, tz, lambda rows: loc[rows, at], lambda rows, v: put(rows, at, v))
                return _

            def put(rows, at, value):
                phi_v[rows, at] = value
                prepare(value, (rows, at))

            lax.fori_loop(0, NX // LANES, add, 0)

        @pl.when(s == STEPS - 1)
        def _():
            def gather(c, _):
                at = lanes(c)
                sums = [cmat[s, r : r + n, at] for r, n in parts(BY, BZ)] + [corn[:, at]]
                zl, zr = fold(sums, ty)
                yl_o[:, at], yr_o[:, at], zl_o[:, at], zr_o[:, at] = sums[0], sums[1], zl, zr
                return _

            lax.fori_loop(0, NX // LANES, gather, 0)

        for n in (0, 4):
            settle(yrecv.at[s, pl.ds(0, NBY - 1)], send_sem.at[s, n])
        for n in (1, 3):
            settle(zrecv.at[s, pl.ds(0, NBZ - 1)], send_sem.at[s, n])
        settle(cy.at[s, pl.ds(0, NBY - 1), pl.ds(0, 2)], send_sem.at[s, 2])
        settle(cz.at[s, pl.ds(0, NBZ - 1), pl.ds(0, 2)], send_sem.at[s, 5])
        return carry

    lax.fori_loop(0, STEPS, step, 0)


def parts(BY, BZ):
    return (0, BZ), (BZ, BZ), (2 * BZ, BY), (2 * BZ + BY, BY)


def fold(sums, ty):
    _, _, zl, zr, corners = sums
    left, right = ty[0][:, 0:LANES], ty[1][:, 0:LANES]
    zl = zl + left * corners[0:1] + right * corners[1:2]
    return zl, zr + left * corners[2:3] + right * corners[3:4]


def expand(BY, BZ, sums, ty, tz, get, put):
    yl, yr = sums[0], sums[1]
    zl, zr = fold(sums, ty)
    left, right = ty[0][:, 0:LANES], ty[1][:, 0:LANES]
    for z in range(BZ):
        rows = slice(z * BY, (z + 1) * BY)
        ends = left * yl[z : z + 1] + right * yr[z : z + 1]
        put(rows, get(rows) + ends + tz[0][z : z + 1, 0:LANES] * zl + tz[1][z : z + 1, 0:LANES] * zr)


def body(NBY, NBZ, phase_field, others, cond_x, cond_y, cond_z, inverse_x, inverse_y, inverse_z):
    BZ, BY, NX = phase_field.shape
    R = BY * BZ
    MR = 2 * BZ + 2 * BY + 16
    KR, KY, KZ = R // 2, NBY * BZ, NBZ * BY
    vmem = pltpu.VMEM
    CW, turns = 256, NX // 256
    call = pl.pallas_call(
        functools.partial(kernel, NBY, NBZ, BY, BZ, NX),
        out_shape=[
            vmem((n, NX), F32) for n in (R, BZ, BZ, BY, BY, BY, BY, BZ, BZ)
        ],
        in_specs=[pl.BlockSpec(memory_space=pl.ANY)] * 5,
        out_specs=[pl.BlockSpec(memory_space=pltpu.VMEM)] * 9,
        scratch_shapes=[
            vmem((R, NX), F32), vmem((R, NX), F32), vmem((turns, CW, CW), F32),
            vmem((max(turns - 1, 1), 16, NX), F32),
            vmem((BY * NBY, BY * NBY), F32), vmem((BY, BY * NBY), F32), vmem((BZ * NBZ, BZ * NBZ), F32),
            vmem((BY, R), F32), vmem((BZ, R), F32),
            vmem((2, turns, CW, CW), BF16), vmem((2, 2 * MR, R), BF16), vmem((2, KR, KR), BF16),
            vmem((2, KR, KR), BF16),
            vmem((2, KY, KY), BF16),
            vmem((2, 16, 8 * NBY), BF16), vmem((2, 8, 8 * NBZ), BF16), vmem((2, KZ, KZ), BF16),
            vmem((2, KZ, KZ), BF16),
            vmem((2, R, NX), BF16), vmem((2, R, NX), BF16), vmem((2, R, NX), BF16),
            vmem((2, MR, NX), BF16), vmem((MR, NX), F32),
            vmem((STEPS, MR, NX), F32), vmem((STEPS, NBY, BZ, LANES), F32),
            vmem((STEPS, NBZ, 2 * BY, LANES), F32), vmem((STEPS, NBY, 8, NX), F32),
            vmem((STEPS, 2, 8, NX), F32), vmem((STEPS, NBZ, 8, NX), F32), vmem((8, NX), F32),
            vmem((STEPS, NBY, BZ, LANES), F32), vmem((STEPS, NBZ, 2 * BY, LANES), F32),
            vmem((STEPS, 2 * BZ + 2 * BY, NX), F32),
            pltpu.SemaphoreType.DMA((2 * turns + 4,)),
            pltpu.SemaphoreType.DMA((STEPS, 6)), pltpu.SemaphoreType.DMA((STEPS, 6)),
        ],
        compiler_params=pltpu.CompilerParams(
            collective_id=0, has_side_effects=True, vmem_limit_bytes=59 << 20
        ),
        name="adi",
    )
    loc, yl, yr, zl, zr, tyl, tyr, tzl, tzr = call(
        phase_field.reshape(R, NX), others.reshape(R, NX), inverse_x, inverse_y, inverse_z
    )
    along_y = tyl[None] * yl[:, None] + tyr[None] * yr[:, None]
    along_z = tzl[:, None] * zl[None] + tzr[:, None] * zr[None]
    return loc.reshape(BZ, BY, NX) + along_y + along_z


def solution(mesh):
    placed = (P("gz", "gy", None), P("gz", "gy", None), P(), P(), P(), P(), P(), P())
    return jax.shard_map(
        functools.partial(body, mesh.shape["gy"], mesh.shape["gz"]),
        mesh=mesh, in_specs=placed, out_specs=P("gz", "gy", None), check_vma=False,
    )
```

```python
import functools

import jax
import jax.numpy as jnp
from jax import lax
from jax.experimental import pallas as pl
from jax.experimental.pallas import tpu as pltpu
from jax.sharding import PartitionSpec as P

STEPS = 2
LANES = 128
F32 = jnp.float32
BF16 = jnp.bfloat16
MESH = pl.DeviceIdType.MESH


def exact(a, b):
    return jnp.dot(a, b, precision=lax.Precision.HIGHEST, preferred_element_type=F32)


def split(x):
    high = x.astype(BF16)
    return high, (x - high.astype(F32)).astype(BF16)


def product(a, b):
    dot = functools.partial(jnp.dot, preferred_element_type=F32)
    return dot(a[0], b[0]) + (dot(a[1], b[0]) + dot(a[0], b[1]))


def rows_of(shape):
    return lax.broadcasted_iota(jnp.int32, shape, 0)


def cols_of(shape):
    return lax.broadcasted_iota(jnp.int32, shape, 1)


def halved(i, bits):
    return lax.shift_right_logical(i, jnp.full_like(i, bits))


def onehot(mask):
    return jnp.where(mask, 1.0, 0.0).astype(F32)


def coarse(inverse, size, blocks):
    width = size * blocks
    at = cols_of((blocks, width)) - rows_of((blocks, width)) * size
    first_rows, last_rows = exact(onehot(at == 0), inverse), exact(onehot(at == size - 1), inverse)
    at = rows_of((width, blocks)) - cols_of((width, blocks)) * size
    first, last = onehot(at == 0), onehot(at == size - 1)
    i, j = rows_of((blocks, blocks)), cols_of((blocks, blocks))
    last_last = jnp.sum(jnp.where(i == j, exact(last_rows, last), 0.0), axis=0, keepdims=True)
    first_first = jnp.sum(jnp.where(i == j, exact(first_rows, first), 0.0), axis=0, keepdims=True)
    left = jnp.where(j < i, exact(first_rows, last) / last_last, 0.0)
    right = jnp.where(j > i, exact(last_rows, first) / first_first, 0.0)
    return left, right


def kernel(
    NBY, NBZ, BY, BZ, NX,
    phi_h, oth_h, gx_h, gy_h, gz_h, loc, yl_o, yr_o, zl_o, zr_o, tyl, tyr, tzl, tzr,
    phi_v, oth_v, gx_v, edge_v, gy_v, gym_v, gz_v, gye_v, gze_v,
    gxs, ms, kz, bdy, kw, cyw, czw, kzl, kzr,
    phs, pss, hs, acs, bb,
    red, yrecv, zrecv, cy, csend, cz, corn, yback, zback, cmat,
    load_sem, field_sem, send_sem, recv_sem,
):
    a, b = lax.axis_index("gy"), lax.axis_index("gz")
    piece, side = a // 2, a % 2
    ty, tz = (tyl, tyr), (tzl, tzr)
    R = BY * BZ
    by, bz = BY.bit_length() - 1, BZ.bit_length() - 1
    YM = 2 * BZ
    CM = YM + 2 * BY
    MR = CM + 16
    CW = 256
    turns = NX // CW

    barrier = pltpu.get_barrier_semaphore()

    def greet_y(k, _):
        pl.semaphore_signal(barrier, inc=1, device_id=((a + k) % NBY, b), device_id_type=MESH)
        return _

    def greet_z(k, _):
        pl.semaphore_signal(barrier, inc=1, device_id=(a, (b + k) % NBZ), device_id_type=MESH)
        return _

    lax.fori_loop(1, NBY, greet_y, 0)
    lax.fori_loop(1, NBZ, greet_z, 0)

    mine = pl.ds(pl.multiple_of(a * BY, BY), BY)
    pairs = [(gy_h.at[mine], gym_v), (gz_h, gz_v)]
    for n in range(turns):
        pairs.append((gx_h.at[pl.ds(n * CW, CW), pl.ds(n * CW, CW)], gx_v.at[n]))
    for n in range(turns - 1):
        pairs.append((gx_h.at[pl.ds((n + 1) * CW - 8, 16)], edge_v.at[n]))
    pairs.append((gy_h, gy_v))
    loads = [pltpu.make_async_copy(s, d, load_sem.at[i]) for i, (s, d) in enumerate(pairs)]
    fields = ((phi_h, phi_v), (oth_h, oth_v))

    def load_field(t, n):
        at = pl.ds(pl.multiple_of(t * CW, CW), CW)
        return pltpu.make_async_copy(fields[n][0].at[:, at], fields[n][1].at[:, at], field_sem.at[t, n])

    for load in loads[0:2]:
        load.start()
    for t in range(turns):
        for n in range(2):
            load_field(t, n).start()
    for load in loads[2:]:
        load.start()
    loads[0].wait()
    loads[1].wait()

    wide = min(LANES, BY * NBY)
    start = (a * BY // wide) * wide
    k, c = rows_of((wide, R)), cols_of((wide, R))
    gye = exact(
        gym_v[:, pl.ds(pl.multiple_of(start, wide), wide)],
        onehot(k == a * BY - start + (c & (BY - 1))),
    )
    k, c = rows_of((BZ * NBZ, R)), cols_of((BZ * NBZ, R))
    gze = exact(gz_v[pl.ds(pl.multiple_of(b * BZ, BZ), BZ), :], onehot(k == b * BZ + halved(c, by)))
    gye_v[...], gze_v[...] = gye, gze
    oz = onehot(rows_of((BZ, R)) == halved(cols_of((BZ, R)), by))
    oy = onehot(rows_of((BY, R)) == (cols_of((BY, R)) & (BY - 1)))
    yl, yf = gye[BY - 1 : BY], gye[0:1]
    zl, zf = gze[BZ - 1 : BZ], gze[0:1]

    def corner(first, second):
        i = rows_of((8, R))
        return jnp.where(i == 0, first, jnp.where(i == 1, second, 0.0))

    m_s = jnp.concatenate(
        [gze * yl, gze * yf, gye * zl, gye * zf, corner(zl * yl, zf * yl), corner(zl * yf, zf * yf)], axis=0
    )
    m_t = jnp.concatenate([oz * yl, oz * yf, oy * zl, oy * zf, jnp.zeros((16, R), F32)], axis=0)
    ms[MR : 2 * MR], ms[2 * MR : 3 * MR] = split(m_s)
    ms[0:MR], ms[3 * MR :] = split(m_t)

    KR = R // 2
    half = BY // 2
    hb = by - 1
    KY, KZ = NBY * BZ, NBZ * BY

    def more_tables():
        loads[-1].wait()
        gye, gze = gye_v[...], gze_v[...]
        tyl[...] = jnp.broadcast_to(gye[:, 0:1] / gye[0:1, 0:1], (BY, NX))
        tyr[...] = jnp.broadcast_to(gye[:, BY - 1 : BY] / gye[BY - 1 : BY, BY - 1 : BY], (BY, NX))
        last = R - BY
        tzl[...] = jnp.broadcast_to(gze[:, 0:1] / gze[0:1, 0:1], (BZ, NX))
        tzr[...] = jnp.broadcast_to(gze[:, last : last + 1] / gze[BZ - 1 : BZ, last : last + 1], (BZ, NX))

        i, j = rows_of((KR, KR)), cols_of((KR, KR))
        tiled = jnp.concatenate([gye[:, 0:KR]] * (KR // BY), axis=0)
        bdy[0], bdy[1] = split(jnp.where(halved(i, by) == halved(j, by), tiled, 0.0))
        k, c = rows_of((BZ * NBZ, KR)), cols_of((BZ * NBZ, KR))
        gzh = exact(gz_v[pl.ds(pl.multiple_of(b * BZ, BZ), BZ), :], onehot(k == b * BZ + halved(c, hb)))
        spread = exact(onehot(halved(rows_of((KR, BZ)), hb) == cols_of((KR, BZ))), gzh)
        kz[0], kz[1] = split(jnp.where((i & (half - 1)) == (j & (half - 1)), spread, 0.0))

        wl, wr = coarse(gy_v[...], BY, NBY)
        w = jnp.where(side == 0, wl, wr)
        i, j = rows_of((KY, KY)), cols_of((KY, KY))
        same = (i & (BZ - 1)) == (j & (BZ - 1))
        down = onehot(halved(rows_of((KY, NBY)), bz) == cols_of((KY, NBY)))
        across = onehot(rows_of((NBY, KY)) == halved(cols_of((NBY, KY)), bz))
        kw[0], kw[1] = split(jnp.where(same, exact(down, exact(w, across)), 0.0))
        mine = onehot(cols_of((16, NBY)) == a)
        across = onehot(rows_of((NBY, 8 * NBY)) == halved(cols_of((NBY, 8 * NBY)), 3))
        i, j = rows_of((16, 8 * NBY)), cols_of((16, 8 * NBY))
        row_l, row_r = exact(exact(mine, wl), across), exact(exact(mine, wr), across)
        value = jnp.where((i & 7) == 0, row_l, jnp.where((i & 7) == 1, row_r, 0.0))
        cyw[0], cyw[1] = split(jnp.where((j & 7) == halved(i, 3), value, 0.0))

        wl, wr = coarse(gz_v[...], BZ, NBZ)
        i, j = rows_of((KZ, KZ)), cols_of((KZ, KZ))
        same = (i & (BY - 1)) == (j & (BY - 1))
        down = onehot(halved(rows_of((KZ, NBZ)), by) == cols_of((KZ, NBZ)))
        across = onehot(rows_of((NBZ, KZ)) == halved(cols_of((NBZ, KZ)), by))
        kzl[0], kzl[1] = split(jnp.where(same, exact(down, exact(wl, across)), 0.0))
        kzr[0], kzr[1] = split(jnp.where(same, exact(down, exact(wr, across)), 0.0))
        mine = onehot(cols_of((8, NBZ)) == b)
        across = onehot(rows_of((NBZ, 8 * NBZ)) == halved(cols_of((NBZ, 8 * NBZ)), 3))
        i, j = rows_of((8, 8 * NBZ)), cols_of((8, 8 * NBZ))
        row_l, row_r = exact(exact(mine, wl), across), exact(exact(mine, wr), across)
        value = jnp.where(i < 2, row_l, jnp.where(i < 4, row_r, 0.0))
        czw[0], czw[1] = split(jnp.where((j & 7) == (i & 1), value, 0.0))

    cy[:, :, 2:8] = jnp.zeros((STEPS, NBY, 6, NX), F32)
    cz[:, :, 2:8] = jnp.zeros((STEPS, NBZ, 6, NX), F32)
    cy[:, a, 0:2] = jnp.zeros((STEPS, 2, NX), F32)
    cz[:, b, 0:2] = jnp.zeros((STEPS, 2, NX), F32)
    def chunk(t):
        return pl.ds(pl.multiple_of(t * CW, CW), CW)

    def lanes(t):
        return pl.ds(pl.multiple_of(t * LANES, LANES), LANES)

    def pair(ref, *at):
        return ref[(0, *at)], ref[(1, *at)]

    def settle(ref, sem):
        pltpu.make_async_copy(ref, ref, sem).wait()

    def along_x(source, target, rows, extra):
        first, last = [], []
        for n in range(turns):
            at = slice(n * CW, (n + 1) * CW)
            part = product((source[0, rows, at], source[1, rows, at]), pair(gxs, n))
            target[rows, at] = part + extra(at)
            first.append(part[:, 0:1])
            last.append(part[:, CW - 1 : CW])
        ups, downs = [None] * turns, [None] * turns
        carry = last[0]
        for n in range(1, turns):
            edge = edge_v[n - 1, 7:8, n * CW : (n + 1) * CW] / edge_v[n - 1, 7:8, n * CW - 1 : n * CW]
            ups[n] = (carry, edge)
            carry = last[n] + carry * edge[:, CW - 1 : CW]
        carry = first[turns - 1]
        for n in range(turns - 2, -1, -1):
            at = (n + 1) * CW
            edge = edge_v[n, 8:9, n * CW : at] / edge_v[n, 8:9, at : at + 1]
            downs[n] = (carry, edge)
            carry = first[n] + carry * edge[:, 0:1]
        for n in range(turns):
            at = slice(n * CW, (n + 1) * CW)
            terms = [p[0] * p[1] for p in (ups[n], downs[n]) if p is not None]
            if terms:
                target[rows, at] += sum(terms[1:], terms[0])

    def prepare(field, at):
        psi = field * (8.0 - 2.0 * field * field - 4.0 * oth_v[at])
        phs[(0, *at)], phs[(1, *at)] = split(field)
        pss[(0, *at)], pss[(1, *at)] = split(psi)

    def step(s, carry):
        def reduce(t, turn):
            at = chunk(t)

            @pl.when(s == 0)
            def _():
                for n in range(2):
                    load_field(t, n).wait()
                prepare(phi_v[:, at], (slice(None), at))

            dot = functools.partial(jnp.dot, preferred_element_type=F32)
            on_field = dot(ms[...], phs[0, :, at])
            on_field_low = dot(ms[0 : 2 * MR], phs[1, :, at])
            on_psi = dot(ms[MR : 3 * MR], pss[0, :, at])
            on_psi_low = dot(ms[MR : 2 * MR], pss[1, :, at])
            first = on_psi[0:MR] + (on_psi[MR:] + on_psi_low)
            second = on_field[0:MR] + (on_field[3 * MR :] + on_field_low[0:MR])
            third = on_field[MR : 2 * MR] + (on_field[2 * MR : 3 * MR] + on_field_low[MR:])
            acs[0, :, at], acs[1, :, at] = split(first - 2.0 * second)
            bb[:, at] = -2.0 * third
            return turn

        lax.fori_loop(0, turns, reduce, 0)

        @pl.when(s == 0)
        def _():
            for load in loads[2:-1]:
                load.wait()
            for n in range(turns):
                gxs[0, n], gxs[1, n] = split(gx_v[n])

        along_x(acs, red.at[s], slice(0, MR), lambda at: bb[:, at])

        @pl.when(s == 0)
        def _():
            pl.semaphore_wait(barrier, NBY + NBZ - 2)

        def send_c(k, _):
            to = (a + k) % NBY
            which = 1 - (to - a + NBY) // NBY
            pltpu.make_async_remote_copy(
                src_ref=red.at[s, pl.ds(pl.multiple_of(CM + 8 * which, 8), 2)],
                dst_ref=cy.at[s, a, pl.ds(0, 2)],
                send_sem=send_sem.at[s, 2], recv_sem=recv_sem.at[s, 2],
                device_id=(to, b), device_id_type=MESH,
            ).start()
            return _

        def send_y(k, _):
            to = (a + k) % NBY
            pltpu.make_async_remote_copy(
                src_ref=red.at[s, pl.ds(pl.multiple_of((to % 2) * BZ, 8), BZ), lanes(to // 2)],
                dst_ref=yrecv.at[s, a],
                send_sem=send_sem.at[s, 0], recv_sem=recv_sem.at[s, 0],
                device_id=(to, b), device_id_type=MESH,
            ).start()
            return _

        def send_z(k, _):
            to = (b + k) % NBZ
            pltpu.make_async_remote_copy(
                src_ref=red.at[s, pl.ds(YM, 2 * BY), lanes(to)],
                dst_ref=zrecv.at[s, b],
                send_sem=send_sem.at[s, 1], recv_sem=recv_sem.at[s, 1],
                device_id=(a, to), device_id_type=MESH,
            ).start()
            return _

        lax.fori_loop(1, NBY, send_c, 0)
        lax.fori_loop(1, NBY, send_y, 0)
        lax.fori_loop(1, NBZ, send_z, 0)
        yrecv[s, a] = red[s, pl.ds(pl.multiple_of(side * BZ, 8), BZ), lanes(piece)]
        zrecv[s, b] = red[s, pl.ds(YM, 2 * BY), lanes(b)]

        def local(t, _):
            at = chunk(t)
            v, w = [], []
            for h in range(2):
                def rows(ref, q):
                    part = ref[q, :, at].reshape(BZ, 2, half, CW)
                    return part[:, h].reshape(KR, CW)

                v.append(product(pair(kz), (rows(phs, 0), rows(phs, 1))).reshape(BZ, half, CW))
                w.append(product(pair(kz), (rows(pss, 0), rows(pss, 1))).reshape(BZ, half, CW))
            v = jnp.concatenate(v, axis=1).reshape(R, CW)
            w = jnp.concatenate(w, axis=1).reshape(R, CW)
            field = phi_v[:, at]
            g = split(w - 2.0 * field)
            vs = split(v)
            for h in range(2):
                at_h = slice(h * KR, (h + 1) * KR)
                first = product(pair(bdy), (g[0][at_h], g[1][at_h]))
                second = product(pair(bdy), (vs[0][at_h], vs[1][at_h]))
                hs[0, at_h, at], hs[1, at_h, at] = split(first - 2.0 * v[at_h])
                loc[at_h, at] = field[at_h] - 2.0 * second
            return _

        early = min(1, turns)

        @pl.when(s == 0)
        def _():
            more_tables()

        @pl.when(s > 0)
        def _():
            lax.fori_loop(0, turns, local, 0)

        @pl.when(s == 0)
        def _():
            lax.fori_loop(0, early, local, 0)

        settle(cy.at[s, pl.ds(0, NBY - 1), pl.ds(0, 2)], recv_sem.at[s, 2])
        csend[s] = product(pair(cyw), split(cy[s].reshape(8 * NBY, NX))).reshape(2, 8, NX)

        def pass_c(k, _):
            to = (b + k) % NBZ
            which = 1 - (to - b + NBZ) // NBZ
            pltpu.make_async_remote_copy(
                src_ref=csend.at[s, which, pl.ds(0, 2)],
                dst_ref=cz.at[s, b, pl.ds(0, 2)],
                send_sem=send_sem.at[s, 5], recv_sem=recv_sem.at[s, 5],
                device_id=(a, to), device_id_type=MESH,
            ).start()
            return _

        lax.fori_loop(1, NBZ, pass_c, 0)

        settle(yrecv.at[s, pl.ds(0, NBY - 1)], recv_sem.at[s, 0])
        yback[s] = product(pair(kw), split(yrecv[s].reshape(KY, LANES))).reshape(NBY, BZ, LANES)

        def return_y(k, _):
            to = (a + k) % NBY
            pltpu.make_async_remote_copy(
                src_ref=yback.at[s, to],
                dst_ref=cmat.at[s, pl.ds(pl.multiple_of(side * BZ, 8), BZ), lanes(piece)],
                send_sem=send_sem.at[s, 4], recv_sem=recv_sem.at[s, 4],
                device_id=(to, b), device_id_type=MESH,
            ).start()
            return _

        lax.fori_loop(1, NBY, return_y, 0)
        cmat[s, pl.ds(pl.multiple_of(side * BZ, 8), BZ), lanes(piece)] = yback[s, a]

        settle(zrecv.at[s, pl.ds(0, NBZ - 1)], recv_sem.at[s, 1])
        for n, matrix in enumerate((kzl, kzr)):
            part = zrecv[s, :, n * BY : (n + 1) * BY].reshape(KZ, LANES)
            zback[s, :, n * BY : (n + 1) * BY] = product(pair(matrix), split(part)).reshape(NBZ, BY, LANES)

        def return_z(k, _):
            to = (b + k) % NBZ
            pltpu.make_async_remote_copy(
                src_ref=zback.at[s, to],
                dst_ref=cmat.at[s, pl.ds(YM, 2 * BY), lanes(b)],
                send_sem=send_sem.at[s, 3], recv_sem=recv_sem.at[s, 3],
                device_id=(a, to), device_id_type=MESH,
            ).start()
            return _

        lax.fori_loop(1, NBZ, return_z, 0)
        cmat[s, pl.ds(YM, 2 * BY), lanes(b)] = zback[s, b]

        @pl.when(s == 0)
        def _():
            lax.fori_loop(early, turns, local, 0)

        def local_x(t, _):
            rows = pl.ds(pl.multiple_of(t * 128, 128), 128)
            along_x(hs, loc, rows, lambda at: loc[rows, at])
            return _

        lax.fori_loop(0, R // 128, local_x, 0)

        settle(cz.at[s, pl.ds(0, NBZ - 1), pl.ds(0, 2)], recv_sem.at[s, 5])
        corn[...] = product(pair(czw), split(cz[s].reshape(8 * NBZ, NX)))
        settle(yrecv.at[s, pl.ds(0, NBY - 1)], recv_sem.at[s, 4])
        settle(zrecv.at[s, pl.ds(0, NBZ - 1)], recv_sem.at[s, 3])

        @pl.when(s < STEPS - 1)
        def _():
            def add(c, _):
                at = lanes(c)
                sums = [cmat[s, r : r + n, at] for r, n in parts(BY, BZ)] + [corn[:, at]]
                expand(BY, BZ, sums, ty, tz, lambda rows: loc[rows, at], lambda rows, v: put(rows, at, v))
                return _

            def put(rows, at, value):
                phi_v[rows, at] = value
                prepare(value, (rows, at))

            lax.fori_loop(0, NX // LANES, add, 0)

        @pl.when(s == STEPS - 1)
        def _():
            def gather(c, _):
                at = lanes(c)
                sums = [cmat[s, r : r + n, at] for r, n in parts(BY, BZ)] + [corn[:, at]]
                zl, zr = fold(sums, ty)
                yl_o[:, at], yr_o[:, at], zl_o[:, at], zr_o[:, at] = sums[0], sums[1], zl, zr
                return _

            lax.fori_loop(0, NX // LANES, gather, 0)

        for n in (0, 4):
            settle(yrecv.at[s, pl.ds(0, NBY - 1)], send_sem.at[s, n])
        for n in (1, 3):
            settle(zrecv.at[s, pl.ds(0, NBZ - 1)], send_sem.at[s, n])
        settle(cy.at[s, pl.ds(0, NBY - 1), pl.ds(0, 2)], send_sem.at[s, 2])
        settle(cz.at[s, pl.ds(0, NBZ - 1), pl.ds(0, 2)], send_sem.at[s, 5])
        return carry

    lax.fori_loop(0, STEPS, step, 0)


def parts(BY, BZ):
    return (0, BZ), (BZ, BZ), (2 * BZ, BY), (2 * BZ + BY, BY)


def fold(sums, ty):
    _, _, zl, zr, corners = sums
    left, right = ty[0][:, 0:LANES], ty[1][:, 0:LANES]
    zl = zl + left * corners[0:1] + right * corners[1:2]
    return zl, zr + left * corners[2:3] + right * corners[3:4]


def expand(BY, BZ, sums, ty, tz, get, put):
    yl, yr = sums[0], sums[1]
    zl, zr = fold(sums, ty)
    left, right = ty[0][:, 0:LANES], ty[1][:, 0:LANES]
    for z in range(BZ):
        rows = slice(z * BY, (z + 1) * BY)
        ends = left * yl[z : z + 1] + right * yr[z : z + 1]
        put(rows, get(rows) + ends + tz[0][z : z + 1, 0:LANES] * zl + tz[1][z : z + 1, 0:LANES] * zr)


def body(NBY, NBZ, phase_field, others, cond_x, cond_y, cond_z, inverse_x, inverse_y, inverse_z):
    BZ, BY, NX = phase_field.shape
    R = BY * BZ
    MR = 2 * BZ + 2 * BY + 16
    KR, KY, KZ = R // 2, NBY * BZ, NBZ * BY
    vmem = pltpu.VMEM
    CW, turns = 256, NX // 256
    call = pl.pallas_call(
        functools.partial(kernel, NBY, NBZ, BY, BZ, NX),
        out_shape=[
            vmem((n, NX), F32) for n in (R, BZ, BZ, BY, BY, BY, BY, BZ, BZ)
        ],
        in_specs=[pl.BlockSpec(memory_space=pl.ANY)] * 5,
        out_specs=[pl.BlockSpec(memory_space=pltpu.VMEM)] * 9,
        scratch_shapes=[
            vmem((R, NX), F32), vmem((R, NX), F32), vmem((turns, CW, CW), F32),
            vmem((max(turns - 1, 1), 16, NX), F32),
            vmem((BY * NBY, BY * NBY), F32), vmem((BY, BY * NBY), F32), vmem((BZ * NBZ, BZ * NBZ), F32),
            vmem((BY, R), F32), vmem((BZ, R), F32),
            vmem((2, turns, CW, CW), BF16), vmem((4 * MR, R), BF16), vmem((2, KR, KR), BF16),
            vmem((2, KR, KR), BF16),
            vmem((2, KY, KY), BF16),
            vmem((2, 16, 8 * NBY), BF16), vmem((2, 8, 8 * NBZ), BF16), vmem((2, KZ, KZ), BF16),
            vmem((2, KZ, KZ), BF16),
            vmem((2, R, NX), BF16), vmem((2, R, NX), BF16), vmem((2, R, NX), BF16),
            vmem((2, MR, NX), BF16), vmem((MR, NX), F32),
            vmem((STEPS, MR, NX), F32), vmem((STEPS, NBY, BZ, LANES), F32),
            vmem((STEPS, NBZ, 2 * BY, LANES), F32), vmem((STEPS, NBY, 8, NX), F32),
            vmem((STEPS, 2, 8, NX), F32), vmem((STEPS, NBZ, 8, NX), F32), vmem((8, NX), F32),
            vmem((STEPS, NBY, BZ, LANES), F32), vmem((STEPS, NBZ, 2 * BY, LANES), F32),
            vmem((STEPS, 2 * BZ + 2 * BY, NX), F32),
            pltpu.SemaphoreType.DMA((2 * turns + 2,)), pltpu.SemaphoreType.DMA((turns, 2)),
            pltpu.SemaphoreType.DMA((STEPS, 6)), pltpu.SemaphoreType.DMA((STEPS, 6)),
        ],
        compiler_params=pltpu.CompilerParams(
            collective_id=0, has_side_effects=True, vmem_limit_bytes=59 << 20
        ),
        name="adi",
    )
    loc, yl, yr, zl, zr, tyl, tyr, tzl, tzr = call(
        phase_field.reshape(R, NX), others.reshape(R, NX), inverse_x, inverse_y, inverse_z
    )
    along_y = tyl[None] * yl[:, None] + tyr[None] * yr[:, None]
    along_z = tzl[:, None] * zl[None] + tzr[:, None] * zr[None]
    return loc.reshape(BZ, BY, NX) + along_y + along_z


def solution(mesh):
    placed = (P("gz", "gy", None), P("gz", "gy", None), P(), P(), P(), P(), P(), P())
    return jax.shard_map(
        functools.partial(body, mesh.shape["gy"], mesh.shape["gz"]),
        mesh=mesh, in_specs=placed, out_specs=P("gz", "gy", None), check_vma=False,
    )
```

```python
import functools

import jax
import jax.numpy as jnp
from jax import lax
from jax.experimental import pallas as pl
from jax.experimental.pallas import tpu as pltpu
from jax.sharding import PartitionSpec as P

STEPS = 2
LANES = 128
F32 = jnp.float32
BF16 = jnp.bfloat16
MESH = pl.DeviceIdType.MESH


def exact(a, b):
    return jnp.dot(a, b, precision=lax.Precision.HIGHEST, preferred_element_type=F32)


def split(x):
    high = x.astype(BF16)
    return high, (x - high.astype(F32)).astype(BF16)


def product(a, b):
    dot = functools.partial(jnp.dot, preferred_element_type=F32)
    return dot(a[0], b[0]) + (dot(a[1], b[0]) + dot(a[0], b[1]))


def rows_of(shape):
    return lax.broadcasted_iota(jnp.int32, shape, 0)


def cols_of(shape):
    return lax.broadcasted_iota(jnp.int32, shape, 1)


def halved(i, bits):
    return lax.shift_right_logical(i, jnp.full_like(i, bits))


def onehot(mask):
    return jnp.where(mask, 1.0, 0.0).astype(F32)


def coarse(inverse, size, blocks):
    width = size * blocks
    at = cols_of((blocks, width)) - rows_of((blocks, width)) * size
    first_rows, last_rows = exact(onehot(at == 0), inverse), exact(onehot(at == size - 1), inverse)
    at = rows_of((width, blocks)) - cols_of((width, blocks)) * size
    first, last = onehot(at == 0), onehot(at == size - 1)
    i, j = rows_of((blocks, blocks)), cols_of((blocks, blocks))
    last_last = jnp.sum(jnp.where(i == j, exact(last_rows, last), 0.0), axis=0, keepdims=True)
    first_first = jnp.sum(jnp.where(i == j, exact(first_rows, first), 0.0), axis=0, keepdims=True)
    left = jnp.where(j < i, exact(first_rows, last) / last_last, 0.0)
    right = jnp.where(j > i, exact(last_rows, first) / first_first, 0.0)
    return left, right


def kernel(
    NBY, NBZ, BY, BZ, NX,
    phi_h, oth_h, gx_h, gy_h, gz_h, loc, yl_o, yr_o, zl_o, zr_o, tyl, tyr, tzl, tzr,
    phi_v, oth_v, gx_v, edge_v, gy_v, gym_v, gz_v, gye_v, gze_v,
    gxs, ms, kz, bdy, kw, cyw, czw, kzl, kzr,
    phs, pss, hs, acs, bb,
    red, yrecv, zrecv, cy, csend, cz, corn, yback, zback, cmat,
    load_sem, field_sem, send_sem, recv_sem,
):
    a, b = lax.axis_index("gy"), lax.axis_index("gz")
    piece, side = a // 2, a % 2
    ty, tz = (tyl, tyr), (tzl, tzr)
    R = BY * BZ
    by, bz = BY.bit_length() - 1, BZ.bit_length() - 1
    YM = 2 * BZ
    CM = YM + 2 * BY
    MR = CM + 16
    CW = 256
    turns = NX // CW

    barrier = pltpu.get_barrier_semaphore()

    def greet_y(k, _):
        pl.semaphore_signal(barrier, inc=1, device_id=((a + k) % NBY, b), device_id_type=MESH)
        return _

    def greet_z(k, _):
        pl.semaphore_signal(barrier, inc=1, device_id=(a, (b + k) % NBZ), device_id_type=MESH)
        return _

    lax.fori_loop(1, NBY, greet_y, 0)
    lax.fori_loop(1, NBZ, greet_z, 0)

    mine = pl.ds(pl.multiple_of(a * BY, BY), BY)
    pairs = [(gy_h.at[mine], gym_v), (gz_h, gz_v)]
    for n in range(turns):
        pairs.append((gx_h.at[pl.ds(n * CW, CW), pl.ds(n * CW, CW)], gx_v.at[n]))
    for n in range(turns - 1):
        pairs.append((gx_h.at[pl.ds((n + 1) * CW - 8, 16)], edge_v.at[n]))
    pairs.append((gy_h, gy_v))
    loads = [pltpu.make_async_copy(s, d, load_sem.at[i]) for i, (s, d) in enumerate(pairs)]
    fields = ((phi_h, phi_v), (oth_h, oth_v))

    def load_field(t, n):
        at = pl.ds(pl.multiple_of(t * CW, CW), CW)
        return pltpu.make_async_copy(fields[n][0].at[:, at], fields[n][1].at[:, at], field_sem.at[t, n])

    for load in loads[0:2]:
        load.start()
    for t in range(turns):
        for n in range(2):
            load_field(t, n).start()
    for load in loads[2:]:
        load.start()
    loads[0].wait()
    loads[1].wait()

    wide = min(LANES, BY * NBY)
    start = (a * BY // wide) * wide
    k, c = rows_of((wide, R)), cols_of((wide, R))
    gye = exact(
        gym_v[:, pl.ds(pl.multiple_of(start, wide), wide)],
        onehot(k == a * BY - start + (c & (BY - 1))),
    )
    k, c = rows_of((BZ * NBZ, R)), cols_of((BZ * NBZ, R))
    gze = exact(gz_v[pl.ds(pl.multiple_of(b * BZ, BZ), BZ), :], onehot(k == b * BZ + halved(c, by)))
    gye_v[...], gze_v[...] = gye, gze
    oz = onehot(rows_of((BZ, R)) == halved(cols_of((BZ, R)), by))
    oy = onehot(rows_of((BY, R)) == (cols_of((BY, R)) & (BY - 1)))
    yl, yf = gye[BY - 1 : BY], gye[0:1]
    zl, zf = gze[BZ - 1 : BZ], gze[0:1]

    def corner(first, second):
        i = rows_of((8, R))
        return jnp.where(i == 0, first, jnp.where(i == 1, second, 0.0))

    m_s = jnp.concatenate(
        [gze * yl, gze * yf, gye * zl, gye * zf, corner(zl * yl, zf * yl), corner(zl * yf, zf * yf)], axis=0
    )
    m_t = jnp.concatenate([oz * yl, oz * yf, oy * zl, oy * zf, jnp.zeros((16, R), F32)], axis=0)
    ms[MR : 2 * MR], ms[2 * MR : 3 * MR] = split(m_s)
    ms[0:MR], ms[3 * MR :] = split(m_t)

    KR = R // 2
    half = BY // 2
    hb = by - 1
    KY, KZ = NBY * BZ, NBZ * BY

    def more_tables():
        loads[-1].wait()
        gye, gze = gye_v[...], gze_v[...]
        tyl[...] = jnp.broadcast_to(gye[:, 0:1] / gye[0:1, 0:1], (BY, NX))
        tyr[...] = jnp.broadcast_to(gye[:, BY - 1 : BY] / gye[BY - 1 : BY, BY - 1 : BY], (BY, NX))
        last = R - BY
        tzl[...] = jnp.broadcast_to(gze[:, 0:1] / gze[0:1, 0:1], (BZ, NX))
        tzr[...] = jnp.broadcast_to(gze[:, last : last + 1] / gze[BZ - 1 : BZ, last : last + 1], (BZ, NX))

        i, j = rows_of((KR, KR)), cols_of((KR, KR))
        tiled = jnp.concatenate([gye[:, 0:KR]] * (KR // BY), axis=0)
        bdy[0], bdy[1] = split(jnp.where(halved(i, by) == halved(j, by), tiled, 0.0))
        k, c = rows_of((BZ * NBZ, KR)), cols_of((BZ * NBZ, KR))
        gzh = exact(gz_v[pl.ds(pl.multiple_of(b * BZ, BZ), BZ), :], onehot(k == b * BZ + halved(c, hb)))
        spread = exact(onehot(halved(rows_of((KR, BZ)), hb) == cols_of((KR, BZ))), gzh)
        kz[0], kz[1] = split(jnp.where((i & (half - 1)) == (j & (half - 1)), spread, 0.0))

        wl, wr = coarse(gy_v[...], BY, NBY)
        w = jnp.where(side == 0, wl, wr)
        i, j = rows_of((KY, KY)), cols_of((KY, KY))
        same = (i & (BZ - 1)) == (j & (BZ - 1))
        down = onehot(halved(rows_of((KY, NBY)), bz) == cols_of((KY, NBY)))
        across = onehot(rows_of((NBY, KY)) == halved(cols_of((NBY, KY)), bz))
        kw[0], kw[1] = split(jnp.where(same, exact(down, exact(w, across)), 0.0))
        mine = onehot(cols_of((16, NBY)) == a)
        across = onehot(rows_of((NBY, 8 * NBY)) == halved(cols_of((NBY, 8 * NBY)), 3))
        i, j = rows_of((16, 8 * NBY)), cols_of((16, 8 * NBY))
        row_l, row_r = exact(exact(mine, wl), across), exact(exact(mine, wr), across)
        value = jnp.where((i & 7) == 0, row_l, jnp.where((i & 7) == 1, row_r, 0.0))
        cyw[0], cyw[1] = split(jnp.where((j & 7) == halved(i, 3), value, 0.0))

        wl, wr = coarse(gz_v[...], BZ, NBZ)
        i, j = rows_of((KZ, KZ)), cols_of((KZ, KZ))
        same = (i & (BY - 1)) == (j & (BY - 1))
        down = onehot(halved(rows_of((KZ, NBZ)), by) == cols_of((KZ, NBZ)))
        across = onehot(rows_of((NBZ, KZ)) == halved(cols_of((NBZ, KZ)), by))
        kzl[0], kzl[1] = split(jnp.where(same, exact(down, exact(wl, across)), 0.0))
        kzr[0], kzr[1] = split(jnp.where(same, exact(down, exact(wr, across)), 0.0))
        mine = onehot(cols_of((8, NBZ)) == b)
        across = onehot(rows_of((NBZ, 8 * NBZ)) == halved(cols_of((NBZ, 8 * NBZ)), 3))
        i, j = rows_of((8, 8 * NBZ)), cols_of((8, 8 * NBZ))
        row_l, row_r = exact(exact(mine, wl), across), exact(exact(mine, wr), across)
        value = jnp.where(i < 2, row_l, jnp.where(i < 4, row_r, 0.0))
        czw[0], czw[1] = split(jnp.where((j & 7) == (i & 1), value, 0.0))

    cy[:, :, 2:8] = jnp.zeros((STEPS, NBY, 6, NX), F32)
    cz[:, :, 2:8] = jnp.zeros((STEPS, NBZ, 6, NX), F32)
    cy[:, a, 0:2] = jnp.zeros((STEPS, 2, NX), F32)
    cz[:, b, 0:2] = jnp.zeros((STEPS, 2, NX), F32)
    def chunk(t):
        return pl.ds(pl.multiple_of(t * CW, CW), CW)

    def lanes(t):
        return pl.ds(pl.multiple_of(t * LANES, LANES), LANES)

    def pair(ref, *at):
        return ref[(0, *at)], ref[(1, *at)]

    def settle(ref, sem):
        pltpu.make_async_copy(ref, ref, sem).wait()

    def along_x(source, target, rows, extra):
        first, last = [], []
        for n in range(turns):
            at = slice(n * CW, (n + 1) * CW)
            part = product((source[0, rows, at], source[1, rows, at]), pair(gxs, n))
            target[rows, at] = part + extra(at)
            first.append(part[:, 0:1])
            last.append(part[:, CW - 1 : CW])
        ups, downs = [None] * turns, [None] * turns
        carry = last[0]
        for n in range(1, turns):
            edge = edge_v[n - 1, 7:8, n * CW : (n + 1) * CW] / edge_v[n - 1, 7:8, n * CW - 1 : n * CW]
            ups[n] = (carry, edge)
            carry = last[n] + carry * edge[:, CW - 1 : CW]
        carry = first[turns - 1]
        for n in range(turns - 2, -1, -1):
            at = (n + 1) * CW
            edge = edge_v[n, 8:9, n * CW : at] / edge_v[n, 8:9, at : at + 1]
            downs[n] = (carry, edge)
            carry = first[n] + carry * edge[:, 0:1]
        for n in range(turns):
            at = slice(n * CW, (n + 1) * CW)
            terms = [p[0] * p[1] for p in (ups[n], downs[n]) if p is not None]
            if terms:
                target[rows, at] += sum(terms[1:], terms[0])

    def prepare(field, at):
        psi = field * (8.0 - 2.0 * field * field - 4.0 * oth_v[at])
        phs[(0, *at)], phs[(1, *at)] = split(field)
        pss[(0, *at)], pss[(1, *at)] = split(psi)

    def step(s, carry):
        def reduce(t, turn):
            at = chunk(t)

            @pl.when(s == 0)
            def _():
                for n in range(2):
                    load_field(t, n).wait()
                prepare(phi_v[:, at], (slice(None), at))

            dot = functools.partial(jnp.dot, preferred_element_type=F32)
            on_field = dot(ms[...], phs[0, :, at])
            on_field_low = dot(ms[0 : 2 * MR], phs[1, :, at])
            on_psi = dot(ms[MR : 3 * MR], pss[0, :, at])
            on_psi_low = dot(ms[MR : 2 * MR], pss[1, :, at])
            first = on_psi[0:MR] + (on_psi[MR:] + on_psi_low)
            second = on_field[0:MR] + (on_field[3 * MR :] + on_field_low[0:MR])
            third = on_field[MR : 2 * MR] + (on_field[2 * MR : 3 * MR] + on_field_low[MR:])
            acs[0, :, at], acs[1, :, at] = split(first - 2.0 * second)
            bb[:, at] = -2.0 * third
            return turn

        lax.fori_loop(0, turns, reduce, 0)

        @pl.when(s == 0)
        def _():
            for load in loads[2:-1]:
                load.wait()
            for n in range(turns):
                gxs[0, n], gxs[1, n] = split(gx_v[n])

        along_x(acs, red.at[s], slice(0, MR), lambda at: bb[:, at])

        @pl.when(s == 0)
        def _():
            pl.semaphore_wait(barrier, NBY + NBZ - 2)

        def send_c(k, _):
            to = (a + k) % NBY
            which = 1 - (to - a + NBY) // NBY
            pltpu.make_async_remote_copy(
                src_ref=red.at[s, pl.ds(pl.multiple_of(CM + 8 * which, 8), 2)],
                dst_ref=cy.at[s, a, pl.ds(0, 2)],
                send_sem=send_sem.at[s, 2], recv_sem=recv_sem.at[s, 2],
                device_id=(to, b), device_id_type=MESH,
            ).start()
            return _

        def send_y(k, _):
            to = (a + k) % NBY
            pltpu.make_async_remote_copy(
                src_ref=red.at[s, pl.ds(pl.multiple_of((to % 2) * BZ, 8), BZ), lanes(to // 2)],
                dst_ref=yrecv.at[s, a],
                send_sem=send_sem.at[s, 0], recv_sem=recv_sem.at[s, 0],
                device_id=(to, b), device_id_type=MESH,
            ).start()
            return _

        def send_z(k, _):
            to = (b + k) % NBZ
            pltpu.make_async_remote_copy(
                src_ref=red.at[s, pl.ds(YM, 2 * BY), lanes(to)],
                dst_ref=zrecv.at[s, b],
                send_sem=send_sem.at[s, 1], recv_sem=recv_sem.at[s, 1],
                device_id=(a, to), device_id_type=MESH,
            ).start()
            return _

        lax.fori_loop(1, NBY, send_c, 0)
        lax.fori_loop(1, NBY, send_y, 0)
        lax.fori_loop(1, NBZ, send_z, 0)
        yrecv[s, a] = red[s, pl.ds(pl.multiple_of(side * BZ, 8), BZ), lanes(piece)]
        zrecv[s, b] = red[s, pl.ds(YM, 2 * BY), lanes(b)]

        def local(t, _):
            at = chunk(t)
            v, w = [], []
            for h in range(2):
                def rows(ref, q):
                    part = ref[q, :, at].reshape(BZ, 2, half, CW)
                    return part[:, h].reshape(KR, CW)

                v.append(product(pair(kz), (rows(phs, 0), rows(phs, 1))).reshape(BZ, half, CW))
                w.append(product(pair(kz), (rows(pss, 0), rows(pss, 1))).reshape(BZ, half, CW))
            v = jnp.concatenate(v, axis=1).reshape(R, CW)
            w = jnp.concatenate(w, axis=1).reshape(R, CW)
            field = phi_v[:, at]
            g = split(w - 2.0 * field)
            vs = split(v)
            for h in range(2):
                at_h = slice(h * KR, (h + 1) * KR)
                first = product(pair(bdy), (g[0][at_h], g[1][at_h]))
                second = product(pair(bdy), (vs[0][at_h], vs[1][at_h]))
                hs[0, at_h, at], hs[1, at_h, at] = split(first - 2.0 * v[at_h])
                loc[at_h, at] = field[at_h] - 2.0 * second
            return _

        early = 0

        @pl.when(s == 0)
        def _():
            more_tables()

        @pl.when(s > 0)
        def _():
            lax.fori_loop(0, turns, local, 0)

        @pl.when(s == 0)
        def _():
            lax.fori_loop(0, early, local, 0)

        settle(cy.at[s, pl.ds(0, NBY - 1), pl.ds(0, 2)], recv_sem.at[s, 2])
        csend[s] = product(pair(cyw), split(cy[s].reshape(8 * NBY, NX))).reshape(2, 8, NX)

        def pass_c(k, _):
            to = (b + k) % NBZ
            which = 1 - (to - b + NBZ) // NBZ
            pltpu.make_async_remote_copy(
                src_ref=csend.at[s, which, pl.ds(0, 2)],
                dst_ref=cz.at[s, b, pl.ds(0, 2)],
                send_sem=send_sem.at[s, 5], recv_sem=recv_sem.at[s, 5],
                device_id=(a, to), device_id_type=MESH,
            ).start()
            return _

        lax.fori_loop(1, NBZ, pass_c, 0)

        settle(yrecv.at[s, pl.ds(0, NBY - 1)], recv_sem.at[s, 0])
        yback[s] = product(pair(kw), split(yrecv[s].reshape(KY, LANES))).reshape(NBY, BZ, LANES)

        def return_y(k, _):
            to = (a + k) % NBY
            pltpu.make_async_remote_copy(
                src_ref=yback.at[s, to],
                dst_ref=cmat.at[s, pl.ds(pl.multiple_of(side * BZ, 8), BZ), lanes(piece)],
                send_sem=send_sem.at[s, 4], recv_sem=recv_sem.at[s, 4],
                device_id=(to, b), device_id_type=MESH,
            ).start()
            return _

        lax.fori_loop(1, NBY, return_y, 0)
        cmat[s, pl.ds(pl.multiple_of(side * BZ, 8), BZ), lanes(piece)] = yback[s, a]

        settle(zrecv.at[s, pl.ds(0, NBZ - 1)], recv_sem.at[s, 1])
        for n, matrix in enumerate((kzl, kzr)):
            part = zrecv[s, :, n * BY : (n + 1) * BY].reshape(KZ, LANES)
            zback[s, :, n * BY : (n + 1) * BY] = product(pair(matrix), split(part)).reshape(NBZ, BY, LANES)

        def return_z(k, _):
            to = (b + k) % NBZ
            pltpu.make_async_remote_copy(
                src_ref=zback.at[s, to],
                dst_ref=cmat.at[s, pl.ds(YM, 2 * BY), lanes(b)],
                send_sem=send_sem.at[s, 3], recv_sem=recv_sem.at[s, 3],
                device_id=(a, to), device_id_type=MESH,
            ).start()
            return _

        lax.fori_loop(1, NBZ, return_z, 0)
        cmat[s, pl.ds(YM, 2 * BY), lanes(b)] = zback[s, b]

        @pl.when(s == 0)
        def _():
            lax.fori_loop(early, turns, local, 0)

        def local_x(t, _):
            rows = pl.ds(pl.multiple_of(t * 128, 128), 128)
            along_x(hs, loc, rows, lambda at: loc[rows, at])
            return _

        lax.fori_loop(0, R // 128, local_x, 0)

        settle(cz.at[s, pl.ds(0, NBZ - 1), pl.ds(0, 2)], recv_sem.at[s, 5])
        corn[...] = product(pair(czw), split(cz[s].reshape(8 * NBZ, NX)))
        settle(yrecv.at[s, pl.ds(0, NBY - 1)], recv_sem.at[s, 4])
        settle(zrecv.at[s, pl.ds(0, NBZ - 1)], recv_sem.at[s, 3])

        @pl.when(s < STEPS - 1)
        def _():
            def add(c, _):
                at = lanes(c)
                sums = [cmat[s, r : r + n, at] for r, n in parts(BY, BZ)] + [corn[:, at]]
                expand(BY, BZ, sums, ty, tz, lambda rows: loc[rows, at], lambda rows, v: put(rows, at, v))
                return _

            def put(rows, at, value):
                phi_v[rows, at] = value
                prepare(value, (rows, at))

            lax.fori_loop(0, NX // LANES, add, 0)

        @pl.when(s == STEPS - 1)
        def _():
            def gather(c, _):
                at = lanes(c)
                sums = [cmat[s, r : r + n, at] for r, n in parts(BY, BZ)] + [corn[:, at]]
                zl, zr = fold(sums, ty)
                yl_o[:, at], yr_o[:, at], zl_o[:, at], zr_o[:, at] = sums[0], sums[1], zl, zr
                return _

            lax.fori_loop(0, NX // LANES, gather, 0)

        for n in (0, 4):
            settle(yrecv.at[s, pl.ds(0, NBY - 1)], send_sem.at[s, n])
        for n in (1, 3):
            settle(zrecv.at[s, pl.ds(0, NBZ - 1)], send_sem.at[s, n])
        settle(cy.at[s, pl.ds(0, NBY - 1), pl.ds(0, 2)], send_sem.at[s, 2])
        settle(cz.at[s, pl.ds(0, NBZ - 1), pl.ds(0, 2)], send_sem.at[s, 5])
        return carry

    lax.fori_loop(0, STEPS, step, 0)


def parts(BY, BZ):
    return (0, BZ), (BZ, BZ), (2 * BZ, BY), (2 * BZ + BY, BY)


def fold(sums, ty):
    _, _, zl, zr, corners = sums
    left, right = ty[0][:, 0:LANES], ty[1][:, 0:LANES]
    zl = zl + left * corners[0:1] + right * corners[1:2]
    return zl, zr + left * corners[2:3] + right * corners[3:4]


def expand(BY, BZ, sums, ty, tz, get, put):
    yl, yr = sums[0], sums[1]
    zl, zr = fold(sums, ty)
    left, right = ty[0][:, 0:LANES], ty[1][:, 0:LANES]
    for z in range(BZ):
        rows = slice(z * BY, (z + 1) * BY)
        ends = left * yl[z : z + 1] + right * yr[z : z + 1]
        put(rows, get(rows) + ends + tz[0][z : z + 1, 0:LANES] * zl + tz[1][z : z + 1, 0:LANES] * zr)


def body(NBY, NBZ, phase_field, others, cond_x, cond_y, cond_z, inverse_x, inverse_y, inverse_z):
    BZ, BY, NX = phase_field.shape
    R = BY * BZ
    MR = 2 * BZ + 2 * BY + 16
    KR, KY, KZ = R // 2, NBY * BZ, NBZ * BY
    vmem = pltpu.VMEM
    CW, turns = 256, NX // 256
    call = pl.pallas_call(
        functools.partial(kernel, NBY, NBZ, BY, BZ, NX),
        out_shape=[
            vmem((n, NX), F32) for n in (R, BZ, BZ, BY, BY, BY, BY, BZ, BZ)
        ],
        in_specs=[pl.BlockSpec(memory_space=pl.ANY)] * 5,
        out_specs=[pl.BlockSpec(memory_space=pltpu.VMEM)] * 9,
        scratch_shapes=[
            vmem((R, NX), F32), vmem((R, NX), F32), vmem((turns, CW, CW), F32),
            vmem((max(turns - 1, 1), 16, NX), F32),
            vmem((BY * NBY, BY * NBY), F32), vmem((BY, BY * NBY), F32), vmem((BZ * NBZ, BZ * NBZ), F32),
            vmem((BY, R), F32), vmem((BZ, R), F32),
            vmem((2, turns, CW, CW), BF16), vmem((4 * MR, R), BF16), vmem((2, KR, KR), BF16),
            vmem((2, KR, KR), BF16),
            vmem((2, KY, KY), BF16),
            vmem((2, 16, 8 * NBY), BF16), vmem((2, 8, 8 * NBZ), BF16), vmem((2, KZ, KZ), BF16),
            vmem((2, KZ, KZ), BF16),
            vmem((2, R, NX), BF16), vmem((2, R, NX), BF16), vmem((2, R, NX), BF16),
            vmem((2, MR, NX), BF16), vmem((MR, NX), F32),
            vmem((STEPS, MR, NX), F32), vmem((STEPS, NBY, BZ, LANES), F32),
            vmem((STEPS, NBZ, 2 * BY, LANES), F32), vmem((STEPS, NBY, 8, NX), F32),
            vmem((STEPS, 2, 8, NX), F32), vmem((STEPS, NBZ, 8, NX), F32), vmem((8, NX), F32),
            vmem((STEPS, NBY, BZ, LANES), F32), vmem((STEPS, NBZ, 2 * BY, LANES), F32),
            vmem((STEPS, 2 * BZ + 2 * BY, NX), F32),
            pltpu.SemaphoreType.DMA((2 * turns + 2,)), pltpu.SemaphoreType.DMA((turns, 2)),
            pltpu.SemaphoreType.DMA((STEPS, 6)), pltpu.SemaphoreType.DMA((STEPS, 6)),
        ],
        compiler_params=pltpu.CompilerParams(
            collective_id=0, has_side_effects=True, vmem_limit_bytes=59 << 20
        ),
        name="adi",
    )
    loc, yl, yr, zl, zr, tyl, tyr, tzl, tzr = call(
        phase_field.reshape(R, NX), others.reshape(R, NX), inverse_x, inverse_y, inverse_z
    )
    along_y = tyl[None] * yl[:, None] + tyr[None] * yr[:, None]
    along_z = tzl[:, None] * zl[None] + tzr[:, None] * zr[None]
    return loc.reshape(BZ, BY, NX) + along_y + along_z


def solution(mesh):
    placed = (P("gz", "gy", None), P("gz", "gy", None), P(), P(), P(), P(), P(), P())
    return jax.shard_map(
        functools.partial(body, mesh.shape["gy"], mesh.shape["gz"]),
        mesh=mesh, in_specs=placed, out_specs=P("gz", "gy", None), check_vma=False,
    )
```
